256 devices in a mesh: ctx: 64 (over x, z, core), ch: 4 (over y).
Axes of the slice: x: 4, y: 4, z: 8, core: 2. Of those that a mesh axis runs over, the one named last changes fastest.
Arguments:
- short_conv_input: bfloat16 [8192, 1024], P('ctx', 'ch'), may hold values from -6 to 6
- out_gate: bfloat16 [8192, 1024], P('ctx', 'ch'), may hold values from -6 to 6
- in_gate: bfloat16 [8192, 1024], P('ctx', 'ch'), may hold values from -6 to 6
- out_cotangent: bfloat16 [8192, 1024], P('ctx', 'ch'), may hold values from -6 to 6
- mr_filter: bfloat16 [128, 64], P(None, 'ch'), may hold values from -0.5 to 0.5
- residues: float32 [16, 1024], P(None, ('ch', 'ctx')), may hold values from -5 to 5
- rates: float32 [16, 1024], P(None, ('ch', 'ctx')), may hold values from 0.00012207031 to 0.03
Outputs:
- input_grad: bfloat16 [8192, 1024], P('ctx', 'ch')
- out_gate_grad: bfloat16 [8192, 1024], P('ctx', 'ch')
- in_gate_grad: bfloat16 [8192, 1024], P('ctx', 'ch')
- filter_grad: float32 [128, 64], P(None, 'ch')
- residue_grad: float32 [16, 1024], P(None, ('ch', 'ctx'))
- rate_grad: float32 [16, 1024], P(None, ('ch', 'ctx'))
The draws below stay inside these ranges and needn't reach their ends.
All inputs are finite; a program needn't handle non-finite values.
Results may differ from the reference program's by a relative error of at most 0.013.
Values may be sent and summed in bfloat16 or wider, within the bound.
No kernel may reach another device: no remote copies, remote signals or barrier semaphores. Data moves between devices by JAX's collectives and lax.ppermute only.
A program may use at most 64 MiB of HBM per device.

```python
import math
import jax
import jax.numpy as jnp
from jax import lax

CHANNELS = 1024
FILTER_TAPS = 128
GROUP = 16
MODES = 16
TOKENS = 8192
GROUPS = 64


def level_of(stream_key, extent, shards, smallest, high):
    gain, own = 1.0, jax.random.fold_in(stream_key, 6)
    for axis_at, blocks in shards:
        heights = jnp.exp(jax.random.uniform(jax.random.fold_in(own, axis_at), (blocks,), jnp.float32, smallest / len(shards), high / len(shards)))
        gain = gain * jnp.repeat(heights, extent[axis_at] // blocks).reshape([-1 if axis == axis_at else 1 for axis in range(len(extent))])
    return gain


def centred(own_key, dims, spread, bound, pieces=(), kind=jnp.bfloat16):
    drawn = spread * jax.random.normal(own_key, dims, jnp.float32)
    if pieces:
        drawn = drawn * level_of(own_key, dims, pieces, -0.22, 0.18)
    return jnp.clip(drawn, -bound, bound).astype(kind)


def setup_inputs(seed: int = 0) -> dict:
    key_of = jax.random.split(jax.random.key(seed), 8)
    short_conv_input = centred(key_of[0], (TOKENS, CHANNELS), 1.0, 6.0, ((0, 64), (1, 4)))
    out_gate = centred(key_of[1], (TOKENS, CHANNELS), 1.0, 6.0, ((0, 64), (1, 4)))
    in_gate = centred(key_of[2], (TOKENS, CHANNELS), 1.0, 6.0, ((0, 64), (1, 4)))
    out_cotangent = centred(key_of[3], (TOKENS, CHANNELS), 1.0, 6.0, ((0, 64), (1, 4)))
    mr_filter = centred(key_of[4], (FILTER_TAPS, GROUPS), FILTER_TAPS ** -0.5, 0.5, ((1, 4),))
    residues = centred(key_of[5], (MODES, CHANNELS), 1.0, 5.0, ((1, 256),), jnp.float32)
    rates = jnp.clip(jnp.exp(math.log(0.03) - 5.5043554 * jax.random.uniform(key_of[6], (MODES, CHANNELS), jnp.float32) ** level_of(key_of[6], (MODES, CHANNELS), ((1, 256),), -0.2, 0.2)), 0.00012207031, 0.03)
    return dict(short_conv_input=short_conv_input, out_gate=out_gate, in_gate=in_gate, out_cotangent=out_cotangent, mr_filter=mr_filter, residues=residues, rates=rates)


def reference(short_conv_input, out_gate, in_gate, out_cotangent, mr_filter, residues, rates):
    single_float = jnp.float32
    bf16 = jnp.bfloat16
    length = short_conv_input.shape[0]
    xf = short_conv_input.astype(single_float)
    gfull = jnp.repeat(mr_filter.astype(single_float), GROUP, axis=1)
    xpad = jnp.concatenate([jnp.zeros((FILTER_TAPS, short_conv_input.shape[1]), single_float), xf], axis=0)

    def add_tap(j, total):
        segment_part = lax.dynamic_slice_in_dim(xpad, (FILTER_TAPS - j).astype(jnp.int32), length, 0)
        return total + gfull[j][None, :] * segment_part
    v = lax.fori_loop(jnp.int32(0), jnp.int32(FILTER_TAPS), add_tap, jnp.zeros(short_conv_input.shape, single_float)).astype(bf16)
    u = (in_gate.astype(single_float) * v.astype(single_float)).astype(bf16)
    dz = (out_gate.astype(single_float) * out_cotangent.astype(single_float)).astype(bf16)
    norm = jnp.sqrt(2.0 * rates / MODES)
    weights = residues * norm
    tau = jnp.arange(length).astype(single_float)

    def add_mode(total, pair):
        weight, rate = pair
        return (total + weight[None, :] * jnp.exp(-rate[None, :] * tau[:, None]), None)
    h, _ = lax.scan(add_mode, jnp.zeros(short_conv_input.shape, single_float), (weights, rates))
    size = 2 * length
    hf = jnp.fft.rfft(h, n=size, axis=0)
    uf = jnp.fft.rfft(u.astype(single_float), n=size, axis=0)
    df = jnp.fft.rfft(dz.astype(single_float), n=size, axis=0)
    z = jnp.fft.irfft(hf * uf, n=size, axis=0)[:length].astype(bf16)
    du = jnp.fft.irfft(jnp.conj(hf) * df, n=size, axis=0)[:length].astype(bf16)
    dh = jnp.fft.irfft(jnp.conj(uf) * df, n=size, axis=0)[:length]
    out_gate_grad = (out_cotangent.astype(single_float) * z.astype(single_float)).astype(bf16)
    in_gate_grad = (du.astype(single_float) * v.astype(single_float)).astype(bf16)
    value_grad = (du.astype(single_float) * in_gate.astype(single_float)).astype(bf16)
    value_grad_full = value_grad.astype(single_float)
    value_grad_padded = jnp.concatenate([value_grad_full, jnp.zeros((FILTER_TAPS, short_conv_input.shape[1]), single_float)], axis=0)

    def add_back(j, total):
        segment_part = lax.dynamic_slice_in_dim(value_grad_padded, j.astype(jnp.int32), length, 0)
        return total + gfull[j][None, :] * segment_part
    input_grad = lax.fori_loop(jnp.int32(0), jnp.int32(FILTER_TAPS), add_back, jnp.zeros(short_conv_input.shape, single_float)).astype(bf16)
    scale = 1.0 / jnp.sqrt(jnp.asarray(length, single_float))

    def tap_sum(j):
        segment_part = lax.dynamic_slice_in_dim(xpad, (FILTER_TAPS - j).astype(jnp.int32), length, 0)
        channel_wise = lax.optimization_barrier(jnp.sum(value_grad_full * segment_part, axis=0))
        return lax.optimization_barrier(jnp.sum(channel_wise.reshape(-1, GROUP), axis=1))
    filter_grad = lax.map(tap_sum, jnp.arange(FILTER_TAPS, dtype=jnp.int32)) * scale

    def mode_sums(rate):
        decay = jnp.exp(-rate[None, :] * tau[:, None])
        first = lax.optimization_barrier(jnp.sum(dh * decay, axis=0))
        second = lax.optimization_barrier(jnp.sum(dh * decay * tau[:, None], axis=0))
        return (first, second)
    s1, s2 = lax.map(mode_sums, rates)
    residue_grad = norm * s1 * scale
    rate_grad = weights * (0.5 * s1 - rates * s2) * scale
    return (input_grad, out_gate_grad, in_gate_grad, filter_grad, residue_grad, rate_grad)
```

```python
import math

import jax
import jax.numpy as jnp
from jax import lax
from jax.experimental import pallas as pl
from jax.experimental.pallas import tpu as pltpu
from jax.sharding import PartitionSpec as P

F32 = jnp.float32
BF16 = jnp.bfloat16
CHUNK = 128
OWN = 4
MODES = 16
LANES = 128
IN_ROWS = 3 * OWN
OUT_ROWS = 3 * OWN + 2
NT = (((1,), (1,)), ((), ()))
TN = (((0,), (0,)), ((), ()))


def dot(left, right, dims=(((1,), (0,)), ((), ()))):
    return lax.dot_general(left, right, dims, preferred_element_type=F32)


def iota(shape, axis):
    return lax.broadcasted_iota(jnp.int32, shape, axis)


def halves(value):
    high = value.astype(BF16)
    return high, (value - high.astype(F32)).astype(BF16)


def rounded(value):
    return value.astype(BF16).astype(F32)


def mirrored(value):
    square = (value.shape[1], value.shape[1])
    flip = (iota(square, 0) + iota(square, 1) == value.shape[1] - 1).astype(BF16)
    return dot(value, flip).astype(BF16)


def diagonal_sums(square):
    rolled = pltpu.roll(square, 1, 1, stride=1, stride_axis=0)
    return jnp.sum(rolled, axis=0, keepdims=True)


def causal(square):
    return iota(square, 0) + iota(square, 1) >= square[0] - 1


def own_lanes(shape, channel):
    return (iota(shape, 1) % (OWN * MODES)) // MODES == channel


def pick_own(table, count):
    total = jnp.zeros((count, LANES), F32)
    for channel in range(OWN):
        part = table[channel * count : (channel + 1) * count]
        total = total + jnp.where(own_lanes(part.shape, channel), part, 0.0)
    return total


def pack_kernel(x_ref, k_ref, q_ref, dy_ref, out_ref):
    gated = rounded(q_ref[...].astype(F32) * dy_ref[...].astype(F32))
    tiles = (x_ref.shape[1] // 8, 8, x_ref.shape[0])
    x = x_ref[...].astype(F32).T.reshape(tiles)
    k = pltpu.roll(k_ref[...].astype(F32).T.reshape(tiles), 4, 1)
    d = gated.T.reshape(tiles)
    low = iota(tiles, 1) < 4
    rows = jnp.stack([jnp.where(low, x, k), jnp.where(low, d, x), jnp.where(low, k, d)], axis=1)
    out_ref[...] = rows.reshape(out_ref.shape).astype(BF16)


def tables_kernel(rates_ref, residues_ref, filt_ref, pick_ref, fwd_ref, bwd_ref, hf_ref, hb_ref,
                  aa_ref, bb_ref, am_ref, bm_ref, g_ref, w_ref, e_ref, lanes_ref):
    def spread(ref):
        return jnp.concatenate(
            [jnp.broadcast_to(ref[:, c : c + 1], (MODES, LANES)) for c in range(OWN)], axis=0
        )

    square = (CHUNK, CHUNK)
    row, lane = iota(square, 0), iota(square, 1)
    upper = lane >= row
    rates, residues = spread(rates_ref), spread(residues_ref)
    weights = residues * jnp.sqrt(2.0 * rates / MODES)
    shape = rates.shape
    step = iota(shape, 1).astype(F32)
    diagonal = iota(shape, 0) == iota(shape, 1) % (OWN * MODES)
    lanes_ref[0:1, :] = jnp.sum(jnp.where(diagonal, rates, 0.0), axis=0, keepdims=True)
    lanes_ref[1:2, :] = jnp.sum(jnp.where(diagonal, residues, 0.0), axis=0, keepdims=True)
    lanes_ref[2:8, :] = jnp.zeros((6, LANES), F32)
    decay = jnp.exp(-rates * step)
    after = jnp.exp(-rates * (step + 1.0))
    before = jnp.exp(-rates * (CHUNK - 1.0 - step))
    e_ref[0 : OWN * MODES, :] = decay
    e_ref[OWN * MODES :, :] = decay * step

    def wide(value):
        high, low = halves(value)
        return jnp.concatenate([jnp.concatenate([high, low], axis=1)] * 2, axis=0)

    aa_ref[...] = wide(before)
    bb_ref[...] = wide(after)
    am_ref[...] = wide(before * (CHUNK - 1.0 - step))
    bm_ref[...] = wide(after * (step + 1.0))

    def tall(value):
        high, low = halves(value)
        return jnp.concatenate([high, high, low, low], axis=0)

    g_ref[...] = tall(weights * after)
    w_ref[...] = tall(weights * before)
    terms = weights * decay
    for c in range(OWN):
        filt = jnp.sum(terms[c * MODES : (c + 1) * MODES], axis=0, keepdims=True)
        band = pltpu.roll(jnp.broadcast_to(filt, square), 0, 1, stride=1, stride_axis=0)
        high, low = halves(jnp.where(upper, band, 0.0))
        hf_ref[c] = jnp.concatenate([high, low], axis=0)
        hb_ref[c] = jnp.concatenate([high, low], axis=1)
    taps = dot(pick_ref[...], filt_ref[...], NT)[0:1]
    band = pltpu.roll(jnp.broadcast_to(taps, square), 0, 1, stride=1, stride_axis=0)
    same = jnp.where(upper, band, 0.0).astype(BF16)
    last = jnp.where(upper, 0.0, band).astype(BF16)
    fwd_ref[...] = jnp.concatenate([same, last], axis=0)
    bwd_ref[...] = jnp.concatenate([same, last], axis=1)


def main_kernel(in_ref, fwd_ref, bwd_ref, hf_ref, hb_ref, aa_ref, bb_ref, g_ref, w_ref, lanes_ref,
                out_ref, u_ref, d_ref, s_ref, in32, out32):
    count = in_ref.shape[0] // IN_ROWS
    rows = OWN * count
    in32[...] = in_ref[...].astype(F32)

    def take(which):
        return jnp.concatenate(
            [in32[pl.ds(which * OWN + c, count, stride=IN_ROWS), :] for c in range(OWN)], axis=0
        )

    def put(which, value):
        for c in range(OWN):
            out32[pl.ds(which * OWN + c, count, stride=OUT_ROWS), :] = value[c * count : (c + 1) * count]

    x, k, d = take(0), take(1), take(2)
    place = iota((rows, CHUNK), 0) % count
    x_last = jnp.where(place == 0, 0.0, pltpu.roll(x, 1, 0))
    xx = jnp.concatenate([x.astype(BF16), x_last.astype(BF16)], axis=1)
    v = rounded(dot(xx, fwd_ref[...]))
    u = (k * v).astype(BF16)
    d = d.astype(BF16)
    u_ref[...] = u
    d_ref[...] = d
    uu = jnp.concatenate([u, u], axis=1)
    dd = jnp.concatenate([d, d], axis=1)
    moment_u = pick_own(dot(uu, aa_ref[...], NT), count)
    moment_d = pick_own(dot(dd, bb_ref[...], NT), count)
    at = iota((count, LANES), 0)
    rates = lanes_ref[0:1, :]
    ahead = jnp.where(at < 1, 0.0, pltpu.roll(moment_u, 1, 0))
    behind = jnp.where(at >= count - 1, 0.0, pltpu.roll(moment_d, count - 1, 0))
    by = 1
    while by < count:
        factor = jnp.exp(rates * (-float(CHUNK) * by))
        ahead = ahead + factor * jnp.where(at < by, 0.0, pltpu.roll(ahead, by, 0))
        behind = behind + factor * jnp.where(at >= count - by, 0.0, pltpu.roll(behind, count - by, 0))
        by *= 2
    s_ref[0] = ahead
    s_ref[1] = behind
    s_ref[2] = moment_d

    def states(value):
        high = rounded(value)
        both = jnp.where(iota(value.shape, 1) < LANES // 2, high, value - high)
        parts = [jnp.where(own_lanes(value.shape, c), both, 0.0) for c in range(OWN)]
        stacked = jnp.concatenate(parts, axis=0).astype(BF16)
        return jnp.concatenate([stacked, stacked], axis=1)

    z = dot(states(ahead), g_ref[...])
    du = dot(states(behind), w_ref[...])
    z_own, du_own = [], []
    for c in range(OWN):
        part = slice(c * count, (c + 1) * count)
        z_own.append(z[part] + dot(uu[part], hf_ref[c]))
        du_own.append(du[part] + dot(dd[part], hb_ref[c], NT))
    put(0, jnp.concatenate(z_own, axis=0))
    du = rounded(jnp.concatenate(du_own, axis=0))
    put(1, du * v)
    dv = rounded(du * k)
    dv_next = jnp.where(place == count - 1, 0.0, pltpu.roll(dv, rows - 1, 0))
    dv = dv.astype(BF16)
    dvv = jnp.concatenate([dv, dv_next.astype(BF16)], axis=1)
    put(2, dot(dvv, bwd_ref[...], NT))
    same = dot(dv, mirrored(xx[:, :CHUNK]), TN)
    last = dot(dv, mirrored(xx[:, CHUNK:]), TN)
    sums = diagonal_sums(jnp.where(causal((CHUNK, CHUNK)), same, last))
    high = rounded(sums)
    out32[pl.ds(3 * OWN, count, stride=OUT_ROWS), :] = jnp.broadcast_to(high, (count, CHUNK))
    out32[pl.ds(3 * OWN + 1, count, stride=OUT_ROWS), :] = jnp.broadcast_to(sums - high, (count, CHUNK))
    out_ref[...] = out32[...].astype(BF16)


def modes_kernel(scale, u_ref, d_ref, s_ref, am_ref, bm_ref, e_ref, lanes_ref, residue_ref, rate_ref):
    count = s_ref.shape[1]
    keep = causal((CHUNK, CHUNK))
    u, d = u_ref[...], d_ref[...]
    u_mirrored = mirrored(u)
    cots = []
    for c in range(OWN):
        part = slice(c * count, (c + 1) * count)
        cots.append(diagonal_sums(jnp.where(keep, dot(d[part], u_mirrored[part], TN), 0.0)))
    cots = jnp.concatenate(cots + [jnp.zeros((8 - OWN, CHUNK), F32)], axis=0)
    inner = lax.dot_general(cots, e_ref[...], NT, precision=lax.Precision.HIGHEST,
                            preferred_element_type=F32)
    inner = jnp.where((iota(inner.shape, 1) % (OWN * MODES)) // MODES == iota(inner.shape, 0), inner, 0.0)
    inner = jnp.sum(inner, axis=0, keepdims=True)
    slope_u = pick_own(dot(jnp.concatenate([u, u], axis=1), am_ref[...], NT), count)
    slope_d = pick_own(dot(jnp.concatenate([d, d], axis=1), bm_ref[...], NT), count)
    rates, residues = lanes_ref[0:1, :], lanes_ref[1:2, :]
    ahead, behind, moment_d = s_ref[0], s_ref[1], s_ref[2]
    first = jnp.sum(ahead * moment_d, axis=0, keepdims=True)
    second = jnp.sum(
        ahead * slope_d + slope_u * behind + (CHUNK * jnp.exp(-CHUNK * rates)) * (ahead * behind),
        axis=0, keepdims=True,
    )
    half = iota((1, LANES), 1) < LANES // 2
    first = first + jnp.where(half, inner, pltpu.roll(inner, LANES // 2, 1))
    second = second + jnp.where(half, pltpu.roll(inner, LANES // 2, 1), inner)
    norm = jnp.sqrt(2.0 * rates / MODES)
    results = ((residue_ref, norm * first * scale),
               (rate_ref, residues * norm * (0.5 * first - rates * second) * scale))
    diagonal = iota((OWN * MODES, LANES), 0) == iota((OWN * MODES, LANES), 1)
    for ref, value in results:
        column = jnp.sum(jnp.where(diagonal, value, 0.0), axis=1, keepdims=True)
        for c in range(OWN):
            ref[:, c : c + 1] = column[c * MODES : (c + 1) * MODES]


def unpack_kernel(scale, in_ref, dy_ref, dx_ref, dq_ref, dk_ref, filt_ref, in32, mid32, sum32):
    count = in_ref.shape[0] // OUT_ROWS
    in32[...] = in_ref[...].astype(F32)

    def take(which):
        for c in range(OWN):
            mid32[which, pl.ds(c, count, stride=OWN), :] = in32[pl.ds(which * OWN + c, count, stride=OUT_ROWS), :]
        return mid32[which].T

    dq_ref[...] = (take(0) * dy_ref[...].astype(F32)).astype(BF16)
    dk_ref[...] = take(1).astype(BF16)
    dx_ref[...] = take(2).astype(BF16)
    sum32[...] = in32[pl.ds(3 * OWN, count, stride=OUT_ROWS), :] + in32[pl.ds(3 * OWN + 1, count, stride=OUT_ROWS), :]
    groups = filt_ref.shape[1]
    share = count // groups
    total = sum32[pl.ds(0, groups, stride=share), :]
    for i in range(1, share):
        total = total + sum32[pl.ds(i, groups, stride=share), :]
    filt_ref[...] = total.T * scale


def shape(dims, kind):
    return jax.ShapeDtypeStruct(dims, kind)


def local(x, out_gate, in_gate, out_cot, mr_filter, residues, rates):
    tokens, chans = x.shape
    peers = lax.axis_size("ctx")
    groups = mr_filter.shape[1]
    scale = 1.0 / math.sqrt(tokens * peers)
    rows = OWN * peers
    square2 = (CHUNK, 2 * CHUNK)
    tall2 = (2 * CHUNK, CHUNK)

    packed = pl.pallas_call(pack_kernel, out_shape=shape((peers * IN_ROWS, CHUNK), BF16), name="pack")(
        x, in_gate, out_gate, out_cot)
    arrived = lax.all_to_all(packed.reshape(3 * peers, OWN, CHUNK), "ctx", split_axis=0, concat_axis=0, tiled=True)

    group = lax.axis_index("ctx") * groups // peers
    pick = (lax.broadcasted_iota(jnp.int32, (8, groups), 1) == group).astype(BF16)
    fwd, bwd, hf, hb, aa, bb, am, bm, g, w, e, lanes = pl.pallas_call(
        tables_kernel,
        out_shape=(
            shape(tall2, BF16), shape(square2, BF16),
            shape((OWN,) + tall2, BF16), shape((OWN,) + square2, BF16),
            shape(square2, BF16), shape(square2, BF16), shape(square2, BF16), shape(square2, BF16),
            shape(tall2, BF16), shape(tall2, BF16),
            shape((LANES, CHUNK), F32), shape((8, LANES), F32),
        ),
        name="tables",
    )(rates, residues, mr_filter, pick)

    back, u, d, states = pl.pallas_call(
        main_kernel,
        out_shape=(shape((peers * OUT_ROWS, CHUNK), BF16), shape((rows, CHUNK), BF16),
                   shape((rows, CHUNK), BF16), shape((3, peers, LANES), F32)),
        scratch_shapes=[pltpu.VMEM((peers * IN_ROWS, CHUNK), F32), pltpu.VMEM((peers * OUT_ROWS, CHUNK), F32)],
        name="mixer",
    )(arrived.reshape(peers * IN_ROWS, CHUNK), fwd, bwd, hf, hb, aa, bb, g, w, lanes)

    returned = lax.all_to_all(back.reshape(peers * OUT_ROWS // 2, 2, CHUNK), "ctx", split_axis=0, concat_axis=0, tiled=True)

    residue_grad, rate_grad = pl.pallas_call(
        lambda *refs: modes_kernel(scale, *refs),
        out_shape=(shape(residues.shape, F32), shape(rates.shape, F32)),
        name="modes",
    )(u, d, states, am, bm, e, lanes)

    input_grad, out_gate_grad, in_gate_grad, filter_grad = pl.pallas_call(
        lambda *refs: unpack_kernel(scale, *refs),
        out_shape=(shape(x.shape, BF16), shape(x.shape, BF16), shape(x.shape, BF16), shape(mr_filter.shape, F32)),
        scratch_shapes=[pltpu.VMEM((peers * OUT_ROWS, CHUNK), F32), pltpu.VMEM((3, chans, CHUNK), F32),
                        pltpu.VMEM((peers, CHUNK), F32)],
        name="unpack",
    )(returned.reshape(peers * OUT_ROWS, CHUNK), out_cot)
    return (input_grad, out_gate_grad, in_gate_grad, filter_grad, residue_grad, rate_grad)


def solution(mesh):
    return jax.shard_map(
        local,
        mesh=mesh,
        in_specs=(
            P("ctx", "ch"),
            P("ctx", "ch"),
            P("ctx", "ch"),
            P("ctx", "ch"),
            P(None, "ch"),
            P(None, ("ch", "ctx")),
            P(None, ("ch", "ctx")),
        ),
        out_specs=(
            P("ctx", "ch"),
            P("ctx", "ch"),
            P("ctx", "ch"),
            P(None, "ch"),
            P(None, ("ch", "ctx")),
            P(None, ("ch", "ctx")),
        ),
        check_vma=False,
    )
```

```python
import math

import jax
import jax.numpy as jnp
from jax import lax
from jax.experimental import pallas as pl
from jax.experimental.pallas import tpu as pltpu
from jax.sharding import PartitionSpec as P

F32 = jnp.float32
BF16 = jnp.bfloat16
CHUNK = 128
OWN = 4
MODES = 16
LANES = 128
IN_ROWS = 3 * OWN
OUT_ROWS = 3 * OWN + 2
NT = (((1,), (1,)), ((), ()))
TN = (((0,), (0,)), ((), ()))


def dot(left, right, dims=(((1,), (0,)), ((), ()))):
    return lax.dot_general(left, right, dims, preferred_element_type=F32)


def iota(shape, axis):
    return lax.broadcasted_iota(jnp.int32, shape, axis)


def halves(value):
    high = value.astype(BF16)
    return high, (value - high.astype(F32)).astype(BF16)


def rounded(value):
    return value.astype(BF16).astype(F32)


def mirrored(value):
    square = (value.shape[1], value.shape[1])
    flip = (iota(square, 0) + iota(square, 1) == value.shape[1] - 1).astype(BF16)
    return dot(value, flip).astype(BF16)


def diagonal_sums(square):
    rolled = pltpu.roll(square, 1, 1, stride=1, stride_axis=0)
    return jnp.sum(rolled, axis=0, keepdims=True)


def causal(square):
    return iota(square, 0) + iota(square, 1) >= square[0] - 1


def own_lanes(shape, channel):
    return (iota(shape, 1) % (OWN * MODES)) // MODES == channel


def pick_own(table, count):
    total = jnp.zeros((count, LANES), F32)
    for channel in range(OWN):
        part = table[channel * count : (channel + 1) * count]
        total = total + jnp.where(own_lanes(part.shape, channel), part, 0.0)
    return total


def pack_kernel(x_ref, k_ref, q_ref, dy_ref, out_ref):
    gated = rounded(q_ref[...].astype(F32) * dy_ref[...].astype(F32))
    tiles = (x_ref.shape[1] // 8, 8, x_ref.shape[0])
    x = x_ref[...].astype(F32).T.reshape(tiles)
    k = pltpu.roll(k_ref[...].astype(F32).T.reshape(tiles), 4, 1)
    d = gated.T.reshape(tiles)
    low = iota(tiles, 1) < 4
    rows = jnp.stack([jnp.where(low, x, k), jnp.where(low, d, x), jnp.where(low, k, d)], axis=1)
    out_ref[...] = rows.reshape(out_ref.shape).astype(BF16)


def tables_kernel(rates_ref, residues_ref, filt_ref, pick_ref, fwd_ref, bwd_ref, hf_ref, hb_ref,
                  aa_ref, bb_ref, am_ref, bm_ref, g_ref, w_ref, e_ref, lanes_ref):
    def spread(ref):
        columns = ref[...].T
        return jnp.concatenate(
            [jnp.broadcast_to(columns[:, c : c + 1], (MODES, LANES)) for c in range(OWN)], axis=0
        )

    square = (CHUNK, CHUNK)
    row, lane = iota(square, 0), iota(square, 1)
    upper = lane >= row
    rates, residues = spread(rates_ref), spread(residues_ref)
    weights = residues * jnp.sqrt(2.0 * rates / MODES)
    shape = rates.shape
    step = iota(shape, 1).astype(F32)
    diagonal = iota(shape, 0) == iota(shape, 1) % (OWN * MODES)
    lanes_ref[0:1, :] = jnp.sum(jnp.where(diagonal, rates, 0.0), axis=0, keepdims=True)
    lanes_ref[1:2, :] = jnp.sum(jnp.where(diagonal, residues, 0.0), axis=0, keepdims=True)
    lanes_ref[2:8, :] = jnp.zeros((6, LANES), F32)
    decay = jnp.exp(-rates * step)
    after = jnp.exp(-rates * (step + 1.0))
    before = jnp.exp(-rates * (CHUNK - 1.0 - step))
    e_ref[0 : OWN * MODES, :] = decay
    e_ref[OWN * MODES :, :] = decay * step

    def wide(value):
        high, low = halves(value)
        return jnp.concatenate([jnp.concatenate([high, low], axis=1)] * 2, axis=0)

    aa_ref[...] = wide(before)
    bb_ref[...] = wide(after)
    am_ref[...] = wide(before * (CHUNK - 1.0 - step))
    bm_ref[...] = wide(after * (step + 1.0))

    def tall(value):
        high, low = halves(value)
        return jnp.concatenate([high, high, low, low], axis=0)

    g_ref[...] = tall(weights * after)
    w_ref[...] = tall(weights * before)
    terms = weights * decay
    for c in range(OWN):
        filt = jnp.sum(terms[c * MODES : (c + 1) * MODES], axis=0, keepdims=True)
        band = pltpu.roll(jnp.broadcast_to(filt, square), 0, 1, stride=1, stride_axis=0)
        high, low = halves(jnp.where(upper, band, 0.0))
        hf_ref[c] = jnp.concatenate([high, low], axis=0)
        hb_ref[c] = jnp.concatenate([high, low], axis=1)
    taps = dot(pick_ref[...], filt_ref[...])[0:1]
    band = pltpu.roll(jnp.broadcast_to(taps, square), 0, 1, stride=1, stride_axis=0)
    same = jnp.where(upper, band, 0.0).astype(BF16)
    last = jnp.where(upper, 0.0, band).astype(BF16)
    fwd_ref[...] = jnp.concatenate([same, last], axis=0)
    bwd_ref[...] = jnp.concatenate([same, last], axis=1)


def main_kernel(in_ref, fwd_ref, bwd_ref, hf_ref, hb_ref, aa_ref, bb_ref, g_ref, w_ref, lanes_ref,
                out_ref, u_ref, d_ref, s_ref, in32, out32):
    count = in_ref.shape[0] // IN_ROWS
    rows = OWN * count
    in32[...] = in_ref[...].astype(F32)

    def take(which):
        return jnp.concatenate(
            [in32[pl.ds(which * OWN + c, count, stride=IN_ROWS), :] for c in range(OWN)], axis=0
        )

    def put(which, value):
        for c in range(OWN):
            out32[pl.ds(which * OWN + c, count, stride=OUT_ROWS), :] = value[c * count : (c + 1) * count]

    x, k, d = take(0), take(1), take(2)
    place = iota((rows, CHUNK), 0) % count
    x_last = jnp.where(place == 0, 0.0, pltpu.roll(x, 1, 0))
    xx = jnp.concatenate([x.astype(BF16), x_last.astype(BF16)], axis=1)
    v = rounded(dot(xx, fwd_ref[...]))
    u = (k * v).astype(BF16)
    d = d.astype(BF16)
    u_ref[...] = u
    d_ref[...] = d
    uu = jnp.concatenate([u, u], axis=1)
    dd = jnp.concatenate([d, d], axis=1)
    moment_u = pick_own(dot(uu, aa_ref[...], NT), count)
    moment_d = pick_own(dot(dd, bb_ref[...], NT), count)
    at = iota((count, LANES), 0)
    rates = lanes_ref[0:1, :]
    ahead = jnp.where(at < 1, 0.0, pltpu.roll(moment_u, 1, 0))
    behind = jnp.where(at >= count - 1, 0.0, pltpu.roll(moment_d, count - 1, 0))
    by = 1
    while by < count:
        factor = jnp.exp(rates * (-float(CHUNK) * by))
        ahead = ahead + factor * jnp.where(at < by, 0.0, pltpu.roll(ahead, by, 0))
        behind = behind + factor * jnp.where(at >= count - by, 0.0, pltpu.roll(behind, count - by, 0))
        by *= 2
    s_ref[0] = ahead
    s_ref[1] = behind
    s_ref[2] = moment_d

    def states(value):
        high = rounded(value)
        both = jnp.where(iota(value.shape, 1) < LANES // 2, high, value - high)
        parts = [jnp.where(own_lanes(value.shape, c), both, 0.0) for c in range(OWN)]
        stacked = jnp.concatenate(parts, axis=0).astype(BF16)
        return jnp.concatenate([stacked, stacked], axis=1)

    z = dot(states(ahead), g_ref[...])
    du = dot(states(behind), w_ref[...])
    z_own, du_own = [], []
    for c in range(OWN):
        part = slice(c * count, (c + 1) * count)
        z_own.append(z[part] + dot(uu[part], hf_ref[c]))
        du_own.append(du[part] + dot(dd[part], hb_ref[c], NT))
    put(0, jnp.concatenate(z_own, axis=0))
    du = rounded(jnp.concatenate(du_own, axis=0))
    put(1, du * v)
    dv = rounded(du * k)
    dv_next = jnp.where(place == count - 1, 0.0, pltpu.roll(dv, rows - 1, 0))
    dv = dv.astype(BF16)
    dvv = jnp.concatenate([dv, dv_next.astype(BF16)], axis=1)
    put(2, dot(dvv, bwd_ref[...], NT))
    same = dot(dv, mirrored(xx[:, :CHUNK]), TN)
    last = dot(dv, mirrored(xx[:, CHUNK:]), TN)
    sums = diagonal_sums(jnp.where(causal((CHUNK, CHUNK)), same, last))
    high = rounded(sums)
    out32[pl.ds(3 * OWN, count, stride=OUT_ROWS), :] = jnp.broadcast_to(high, (count, CHUNK))
    out32[pl.ds(3 * OWN + 1, count, stride=OUT_ROWS), :] = jnp.broadcast_to(sums - high, (count, CHUNK))
    out_ref[...] = out32[...].astype(BF16)


def modes_kernel(scale, u_ref, d_ref, s_ref, am_ref, bm_ref, e_ref, lanes_ref, residue_ref, rate_ref):
    count = s_ref.shape[1]
    keep = causal((CHUNK, CHUNK))
    u, d = u_ref[...], d_ref[...]
    u_mirrored = mirrored(u)
    cots = []
    for c in range(OWN):
        part = slice(c * count, (c + 1) * count)
        cots.append(diagonal_sums(jnp.where(keep, dot(d[part], u_mirrored[part], TN), 0.0)))
    cots = jnp.concatenate(cots + [jnp.zeros((8 - OWN, CHUNK), F32)], axis=0)
    inner = lax.dot_general(cots, e_ref[...], NT, precision=lax.Precision.HIGHEST,
                            preferred_element_type=F32)
    inner = jnp.where((iota(inner.shape, 1) % (OWN * MODES)) // MODES == iota(inner.shape, 0), inner, 0.0)
    inner = jnp.sum(inner, axis=0, keepdims=True)
    slope_u = pick_own(dot(jnp.concatenate([u, u], axis=1), am_ref[...], NT), count)
    slope_d = pick_own(dot(jnp.concatenate([d, d], axis=1), bm_ref[...], NT), count)
    rates, residues = lanes_ref[0:1, :], lanes_ref[1:2, :]
    ahead, behind, moment_d = s_ref[0], s_ref[1], s_ref[2]
    first = jnp.sum(ahead * moment_d, axis=0, keepdims=True)
    second = jnp.sum(
        ahead * slope_d + slope_u * behind + (CHUNK * jnp.exp(-CHUNK * rates)) * (ahead * behind),
        axis=0, keepdims=True,
    )
    half = iota((1, LANES), 1) < LANES // 2
    first = first + jnp.where(half, inner, pltpu.roll(inner, LANES // 2, 1))
    second = second + jnp.where(half, pltpu.roll(inner, LANES // 2, 1), inner)
    norm = jnp.sqrt(2.0 * rates / MODES)
    results = ((residue_ref, norm * first * scale),
               (rate_ref, residues * norm * (0.5 * first - rates * second) * scale))
    for ref, value in results:
        for c in range(OWN):
            ref[c : c + 1, :] = value[:, c * MODES : (c + 1) * MODES]


def unpack_kernel(scale, in_ref, dy_ref, dx_ref, dq_ref, dk_ref, filt_ref, in32, mid32, sum32):
    count = in_ref.shape[0] // OUT_ROWS
    in32[...] = in_ref[...].astype(F32)

    def take(which):
        for c in range(OWN):
            mid32[which, pl.ds(c, count, stride=OWN), :] = in32[pl.ds(which * OWN + c, count, stride=OUT_ROWS), :]
        return mid32[which].T

    dq_ref[...] = (take(0) * dy_ref[...].astype(F32)).astype(BF16)
    dk_ref[...] = take(1).astype(BF16)
    dx_ref[...] = take(2).astype(BF16)
    sum32[...] = in32[pl.ds(3 * OWN, count, stride=OUT_ROWS), :] + in32[pl.ds(3 * OWN + 1, count, stride=OUT_ROWS), :]
    groups = filt_ref.shape[0]
    share = count // groups
    total = sum32[pl.ds(0, groups, stride=share), :]
    for i in range(1, share):
        total = total + sum32[pl.ds(i, groups, stride=share), :]
    filt_ref[...] = total * scale


ROOM = pltpu.CompilerParams(vmem_limit_bytes=8 * 1024 * 1024)


def shape(dims, kind):
    return jax.ShapeDtypeStruct(dims, kind)


def local(x, out_gate, in_gate, out_cot, mr_filter, residues, rates):
    tokens, chans = x.shape
    peers = lax.axis_size("ctx")
    groups = mr_filter.shape[1]
    scale = 1.0 / math.sqrt(tokens * peers)
    rows = OWN * peers
    square2 = (CHUNK, 2 * CHUNK)
    tall2 = (2 * CHUNK, CHUNK)

    packed = pl.pallas_call(pack_kernel, out_shape=shape((peers * IN_ROWS, CHUNK), BF16), name="pack")(
        x, in_gate, out_gate, out_cot)
    arrived = lax.all_to_all(packed.reshape(3 * peers, OWN, CHUNK), "ctx", split_axis=0, concat_axis=0, tiled=True)

    group = lax.axis_index("ctx") * groups // peers
    pick = (lax.broadcasted_iota(jnp.int32, (8, groups), 1) == group).astype(BF16)
    fwd, bwd, hf, hb, aa, bb, am, bm, g, w, e, lanes = pl.pallas_call(
        tables_kernel,
        out_shape=(
            shape(tall2, BF16), shape(square2, BF16),
            shape((OWN,) + tall2, BF16), shape((OWN,) + square2, BF16),
            shape(square2, BF16), shape(square2, BF16), shape(square2, BF16), shape(square2, BF16),
            shape(tall2, BF16), shape(tall2, BF16),
            shape((LANES, CHUNK), F32), shape((8, LANES), F32),
        ),
        compiler_params=ROOM, name="tables",
    )(rates.T, residues.T, mr_filter.T, pick)

    back, u, d, states = pl.pallas_call(
        main_kernel,
        out_shape=(shape((peers * OUT_ROWS, CHUNK), BF16), shape((rows, CHUNK), BF16),
                   shape((rows, CHUNK), BF16), shape((3, peers, LANES), F32)),
        scratch_shapes=[pltpu.VMEM((peers * IN_ROWS, CHUNK), F32), pltpu.VMEM((peers * OUT_ROWS, CHUNK), F32)],
        compiler_params=ROOM, name="mixer",
    )(arrived.reshape(peers * IN_ROWS, CHUNK), fwd, bwd, hf, hb, aa, bb, g, w, lanes)

    returned = lax.all_to_all(back.reshape(peers * OUT_ROWS // 2, 2, CHUNK), "ctx", split_axis=0, concat_axis=0, tiled=True)

    residue_grad, rate_grad = pl.pallas_call(
        lambda *refs: modes_kernel(scale, *refs),
        out_shape=(shape(residues.shape[::-1], F32), shape(rates.shape[::-1], F32)),
        compiler_params=ROOM, name="modes",
    )(u, d, states, am, bm, e, lanes)

    input_grad, out_gate_grad, in_gate_grad, filter_grad = pl.pallas_call(
        lambda *refs: unpack_kernel(scale, *refs),
        out_shape=(shape(x.shape, BF16), shape(x.shape, BF16), shape(x.shape, BF16), shape(mr_filter.shape[::-1], F32)),
        scratch_shapes=[pltpu.VMEM((peers * OUT_ROWS, CHUNK), F32), pltpu.VMEM((3, chans, CHUNK), F32),
                        pltpu.VMEM((peers, CHUNK), F32)],
        compiler_params=ROOM, name="unpack",
    )(returned.reshape(peers * OUT_ROWS, CHUNK), out_cot)
    return (input_grad, out_gate_grad, in_gate_grad, filter_grad.T, residue_grad.T, rate_grad.T)


def solution(mesh):
    return jax.shard_map(
        local,
        mesh=mesh,
        in_specs=(
            P("ctx", "ch"),
            P("ctx", "ch"),
            P("ctx", "ch"),
            P("ctx", "ch"),
            P(None, "ch"),
            P(None, ("ch", "ctx")),
            P(None, ("ch", "ctx")),
        ),
        out_specs=(
            P("ctx", "ch"),
            P("ctx", "ch"),
            P("ctx", "ch"),
            P(None, "ch"),
            P(None, ("ch", "ctx")),
            P(None, ("ch", "ctx")),
        ),
        check_vma=False,
    )
```

```python
import math

import jax
import jax.numpy as jnp
from jax import lax
from jax.experimental import pallas as pl
from jax.experimental.pallas import tpu as pltpu
from jax.sharding import PartitionSpec as P

F32 = jnp.float32
BF16 = jnp.bfloat16
CHUNK = 128
OWN = 4
MODES = 16
LANES = 128
IN_ROWS = 3 * OWN
OUT_ROWS = 3 * OWN + 2
NT = (((1,), (1,)), ((), ()))
TN = (((0,), (0,)), ((), ()))


def dot(left, right, dims=(((1,), (0,)), ((), ()))):
    return lax.dot_general(left, right, dims, preferred_element_type=F32)


def iota(shape, axis):
    return lax.broadcasted_iota(jnp.int32, shape, axis)


def halves(value):
    high = value.astype(BF16)
    return high, (value - high.astype(F32)).astype(BF16)


def rounded(value):
    return value.astype(BF16).astype(F32)


def mirrored(value):
    square = (value.shape[1], value.shape[1])
    flip = (iota(square, 0) + iota(square, 1) == value.shape[1] - 1).astype(BF16)
    return dot(value, flip).astype(BF16)


def diagonal_sums(square):
    rolled = pltpu.roll(square, 1, 1, stride=1, stride_axis=0)
    return jnp.sum(rolled, axis=0, keepdims=True)


def causal(square):
    return iota(square, 0) + iota(square, 1) >= square[0] - 1


def own_lanes(shape, channel):
    return (iota(shape, 1) % (OWN * MODES)) // MODES == channel


def pick_own(table, count):
    total = jnp.zeros((count, LANES), F32)
    for channel in range(OWN):
        part = table[channel * count : (channel + 1) * count]
        total = total + jnp.where(own_lanes(part.shape, channel), part, 0.0)
    return total


def pack_into(x, k, q, dy, out_ref):
    tiles = (x.shape[1] // 8, 8, x.shape[0])
    gated = rounded(q.astype(F32) * dy.astype(F32))
    x = x.astype(F32).T.reshape(tiles)
    k = pltpu.roll(k.astype(F32).T.reshape(tiles), 4, 1)
    d = gated.T.reshape(tiles)
    low = iota(tiles, 1) < 4
    rows = jnp.stack([jnp.where(low, x, k), jnp.where(low, d, x), jnp.where(low, k, d)], axis=1)
    out_ref[...] = rows.reshape(out_ref.shape).astype(BF16)


def front_kernel(*refs):
    sources, results, held, done = refs[:7], refs[7:20], refs[20:27], refs[27]
    copies = [pltpu.make_async_copy(sources[i], held[i], done.at[i]) for i in range(len(sources))]
    for copy in copies:
        copy.start()
    for copy in copies:
        copy.wait()
    x_ref, k_ref, q_ref, dy_ref, rates_ref, residues_ref, filt_ref = held
    (out_ref, fwd_ref, bwd_ref, hf_ref, hb_ref, aa_ref, bb_ref, am_ref, bm_ref, g_ref, w_ref,
     e_ref, lanes_ref) = results
    pack_into(x_ref[...], k_ref[...], q_ref[...], dy_ref[...], out_ref)

    def spread(ref):
        columns = ref[...].T
        return jnp.concatenate(
            [jnp.broadcast_to(columns[:, c : c + 1], (MODES, LANES)) for c in range(OWN)], axis=0
        )

    square = (CHUNK, CHUNK)
    row, lane = iota(square, 0), iota(square, 1)
    upper = lane >= row
    rates, residues = spread(rates_ref), spread(residues_ref)
    weights = residues * jnp.sqrt(2.0 * rates / MODES)
    shape = rates.shape
    step = iota(shape, 1).astype(F32)
    diagonal = iota(shape, 0) == iota(shape, 1) % (OWN * MODES)
    lanes_ref[0:1, :] = jnp.sum(jnp.where(diagonal, rates, 0.0), axis=0, keepdims=True)
    lanes_ref[1:2, :] = jnp.sum(jnp.where(diagonal, residues, 0.0), axis=0, keepdims=True)
    lanes_ref[2:8, :] = jnp.zeros((6, LANES), F32)
    decay = jnp.exp(-rates * step)
    after = jnp.exp(-rates * (step + 1.0))
    before = jnp.exp(-rates * (CHUNK - 1.0 - step))
    e_ref[0 : OWN * MODES, :] = decay
    e_ref[OWN * MODES :, :] = decay * step

    def wide(value):
        high, low = halves(value)
        return jnp.concatenate([jnp.concatenate([high, low], axis=1)] * 2, axis=0)

    aa_ref[...] = wide(before)
    bb_ref[...] = wide(after)
    am_ref[...] = wide(before * (CHUNK - 1.0 - step))
    bm_ref[...] = wide(after * (step + 1.0))

    def tall(value):
        high, low = halves(value)
        return jnp.concatenate([high, high, low, low], axis=0)

    g_ref[...] = tall(weights * after)
    w_ref[...] = tall(weights * before)
    terms = weights * decay
    for c in range(OWN):
        filt = jnp.sum(terms[c * MODES : (c + 1) * MODES], axis=0, keepdims=True)
        band = pltpu.roll(jnp.broadcast_to(filt, square), 0, 1, stride=1, stride_axis=0)
        high, low = halves(jnp.where(upper, band, 0.0))
        hf_ref[c] = jnp.concatenate([high, low], axis=0)
        hb_ref[c] = jnp.concatenate([high, low], axis=1)
    share = lax.axis_size("ctx") // filt_ref.shape[0]
    group = lax.axis_index("ctx") // share
    pick = (iota((8, filt_ref.shape[0]), 1) == group).astype(BF16)
    taps = dot(pick, filt_ref[...])[0:1]
    band = pltpu.roll(jnp.broadcast_to(taps, square), 0, 1, stride=1, stride_axis=0)
    same = jnp.where(upper, band, 0.0).astype(BF16)
    last = jnp.where(upper, 0.0, band).astype(BF16)
    fwd_ref[...] = jnp.concatenate([same, last], axis=0)
    bwd_ref[...] = jnp.concatenate([same, last], axis=1)


def main_kernel(in_ref, fwd_ref, bwd_ref, hf_ref, hb_ref, aa_ref, bb_ref, am_ref, bm_ref, g_ref, w_ref,
                e_ref, lanes_ref, out_ref, sums_ref, in32, out32):
    count = in_ref.shape[0] // IN_ROWS
    rows = OWN * count
    in32[...] = in_ref[...].astype(F32)

    def take(which):
        return jnp.concatenate(
            [in32[pl.ds(which * OWN + c, count, stride=IN_ROWS), :] for c in range(OWN)], axis=0
        )

    def put(which, value):
        for c in range(OWN):
            out32[pl.ds(which * OWN + c, count, stride=OUT_ROWS), :] = value[c * count : (c + 1) * count]

    x, k, d = take(0), take(1), take(2)
    place = iota((rows, CHUNK), 0) % count
    x_last = jnp.where(place == 0, 0.0, pltpu.roll(x, 1, 0))
    xx = jnp.concatenate([x.astype(BF16), x_last.astype(BF16)], axis=1)
    v = rounded(dot(xx, fwd_ref[...]))
    u = (k * v).astype(BF16)
    d = d.astype(BF16)
    uu = jnp.concatenate([u, u], axis=1)
    dd = jnp.concatenate([d, d], axis=1)
    moment_u = pick_own(dot(uu, aa_ref[...], NT), count)
    moment_d = pick_own(dot(dd, bb_ref[...], NT), count)
    at = iota((count, LANES), 0)
    rates = lanes_ref[0:1, :]
    ahead = jnp.where(at < 1, 0.0, pltpu.roll(moment_u, 1, 0))
    behind = jnp.where(at >= count - 1, 0.0, pltpu.roll(moment_d, count - 1, 0))
    by = 1
    while by < count:
        factor = jnp.exp(rates * (-float(CHUNK) * by))
        ahead = ahead + factor * jnp.where(at < by, 0.0, pltpu.roll(ahead, by, 0))
        behind = behind + factor * jnp.where(at >= count - by, 0.0, pltpu.roll(behind, count - by, 0))
        by *= 2

    def states(value):
        high = rounded(value)
        both = jnp.where(iota(value.shape, 1) < LANES // 2, high, value - high)
        parts = [jnp.where(own_lanes(value.shape, c), both, 0.0) for c in range(OWN)]
        stacked = jnp.concatenate(parts, axis=0).astype(BF16)
        return jnp.concatenate([stacked, stacked], axis=1)

    z = dot(states(ahead), g_ref[...])
    du = dot(states(behind), w_ref[...])
    z_own, du_own = [], []
    for c in range(OWN):
        part = slice(c * count, (c + 1) * count)
        z_own.append(z[part] + dot(uu[part], hf_ref[c]))
        du_own.append(du[part] + dot(dd[part], hb_ref[c], NT))
    put(0, jnp.concatenate(z_own, axis=0))
    du = rounded(jnp.concatenate(du_own, axis=0))
    put(1, du * v)
    dv = rounded(du * k)
    dv_next = jnp.where(place == count - 1, 0.0, pltpu.roll(dv, rows - 1, 0))
    dv = dv.astype(BF16)
    dvv = jnp.concatenate([dv, dv_next.astype(BF16)], axis=1)
    put(2, dot(dvv, bwd_ref[...], NT))
    same = dot(dv, mirrored(xx[:, :CHUNK]), TN)
    last = dot(dv, mirrored(xx[:, CHUNK:]), TN)
    sums = diagonal_sums(jnp.where(causal((CHUNK, CHUNK)), same, last))
    high = rounded(sums)
    out32[pl.ds(3 * OWN, count, stride=OUT_ROWS), :] = jnp.broadcast_to(high, (count, CHUNK))
    out32[pl.ds(3 * OWN + 1, count, stride=OUT_ROWS), :] = jnp.broadcast_to(sums - high, (count, CHUNK))
    out_ref[...] = out32[...].astype(BF16)
    first, second = mode_sums(u, d, ahead, behind, moment_d, am_ref, bm_ref, e_ref, lanes_ref)
    sums_ref[...] = jnp.concatenate([first, second, jnp.zeros((6, LANES), F32)], axis=0)


def mode_sums(u, d, ahead, behind, moment_d, am_ref, bm_ref, e_ref, lanes_ref):
    count = ahead.shape[0]
    keep = causal((CHUNK, CHUNK))
    u_mirrored = mirrored(u)
    cots = []
    for c in range(OWN):
        part = slice(c * count, (c + 1) * count)
        cots.append(diagonal_sums(jnp.where(keep, dot(d[part], u_mirrored[part], TN), 0.0)))
    cots = jnp.concatenate(cots + [jnp.zeros((8 - OWN, CHUNK), F32)], axis=0)
    inner = lax.dot_general(cots, e_ref[...], NT, precision=lax.Precision.HIGHEST,
                            preferred_element_type=F32)
    inner = jnp.where((iota(inner.shape, 1) % (OWN * MODES)) // MODES == iota(inner.shape, 0), inner, 0.0)
    inner = jnp.sum(inner, axis=0, keepdims=True)
    slope_u = pick_own(dot(jnp.concatenate([u, u], axis=1), am_ref[...], NT), count)
    slope_d = pick_own(dot(jnp.concatenate([d, d], axis=1), bm_ref[...], NT), count)
    rates = lanes_ref[0:1, :]
    first = jnp.sum(ahead * moment_d, axis=0, keepdims=True)
    second = jnp.sum(
        ahead * slope_d + slope_u * behind + (CHUNK * jnp.exp(-CHUNK * rates)) * (ahead * behind),
        axis=0, keepdims=True,
    )
    half = iota((1, LANES), 1) < LANES // 2
    first = first + jnp.where(half, inner, pltpu.roll(inner, LANES // 2, 1))
    second = second + jnp.where(half, pltpu.roll(inner, LANES // 2, 1), inner)
    return first, second


def mode_results(scale, sums_ref, lanes_ref, residue_ref, rate_ref):
    first, second = sums_ref[0:1, :], sums_ref[1:2, :]
    rates, residues = lanes_ref[0:1, :], lanes_ref[1:2, :]
    norm = jnp.sqrt(2.0 * rates / MODES)
    results = ((residue_ref, norm * first * scale),
               (rate_ref, residues * norm * (0.5 * first - rates * second) * scale))
    for ref, value in results:
        for c in range(OWN):
            ref[c : c + 1, :] = value[:, c * MODES : (c + 1) * MODES]


def unpack_kernel(scale, in_ref, dy_ref, sums_ref, lanes_ref, dx_ref, dq_ref, dk_ref, filt_ref,
                  residue_ref, rate_ref, in32, mid32, sum32):
    mode_results(scale, sums_ref, lanes_ref, residue_ref, rate_ref)
    count = in_ref.shape[0] // OUT_ROWS
    in32[...] = in_ref[...].astype(F32)

    def take(which):
        for c in range(OWN):
            mid32[which, pl.ds(c, count, stride=OWN), :] = in32[pl.ds(which * OWN + c, count, stride=OUT_ROWS), :]
        return mid32[which].T

    dq_ref[...] = (take(0) * dy_ref[...].astype(F32)).astype(BF16)
    dk_ref[...] = take(1).astype(BF16)
    dx_ref[...] = take(2).astype(BF16)
    sum32[...] = in32[pl.ds(3 * OWN, count, stride=OUT_ROWS), :] + in32[pl.ds(3 * OWN + 1, count, stride=OUT_ROWS), :]
    groups = filt_ref.shape[0]
    share = count // groups
    total = sum32[pl.ds(0, groups, stride=share), :]
    for i in range(1, share):
        total = total + sum32[pl.ds(i, groups, stride=share), :]
    filt_ref[...] = total * scale


ROOM = pltpu.CompilerParams(vmem_limit_bytes=8 * 1024 * 1024)


def shape(dims, kind):
    return jax.ShapeDtypeStruct(dims, kind)


def local(x, out_gate, in_gate, out_cot, mr_filter, residues, rates):
    tokens, chans = x.shape
    peers = lax.axis_size("ctx")
    scale = 1.0 / math.sqrt(tokens * peers)
    square2 = (CHUNK, 2 * CHUNK)
    tall2 = (2 * CHUNK, CHUNK)

    sources = (x, in_gate, out_gate, out_cot, rates.T, residues.T, mr_filter.T)
    packed, fwd, bwd, hf, hb, aa, bb, am, bm, g, w, e, lanes = pl.pallas_call(
        front_kernel,
        out_shape=(
            shape((peers * IN_ROWS, CHUNK), BF16), shape(tall2, BF16), shape(square2, BF16),
            shape((OWN,) + tall2, BF16), shape((OWN,) + square2, BF16),
            shape(square2, BF16), shape(square2, BF16), shape(square2, BF16), shape(square2, BF16),
            shape(tall2, BF16), shape(tall2, BF16),
            shape((LANES, CHUNK), F32), shape((8, LANES), F32),
        ),
        in_specs=[pl.BlockSpec(memory_space=pltpu.HBM)] * len(sources),
        scratch_shapes=[pltpu.VMEM(source.shape, source.dtype) for source in sources]
        + [pltpu.SemaphoreType.DMA((len(sources),))],
        compiler_params=ROOM, name="front",
    )(*[pltpu.with_memory_space_constraint(source, pltpu.HBM) for source in sources])
    arrived = lax.all_to_all(packed.reshape(3 * peers, OWN, CHUNK), "ctx", split_axis=0, concat_axis=0, tiled=True)

    back, sums = pl.pallas_call(
        main_kernel,
        out_shape=(shape((peers * OUT_ROWS, CHUNK), BF16), shape((8, LANES), F32)),
        scratch_shapes=[pltpu.VMEM((peers * IN_ROWS, CHUNK), F32), pltpu.VMEM((peers * OUT_ROWS, CHUNK), F32)],
        compiler_params=ROOM, name="mixer",
    )(arrived.reshape(peers * IN_ROWS, CHUNK), fwd, bwd, hf, hb, aa, bb, am, bm, g, w, e, lanes)

    returned = lax.all_to_all(back.reshape(peers * OUT_ROWS // 2, 2, CHUNK), "ctx", split_axis=0, concat_axis=0, tiled=True)

    input_grad, out_gate_grad, in_gate_grad, filter_grad, residue_grad, rate_grad = pl.pallas_call(
        lambda *refs: unpack_kernel(scale, *refs),
        out_shape=(shape(x.shape, BF16), shape(x.shape, BF16), shape(x.shape, BF16),
                   shape(mr_filter.shape[::-1], F32),
                   shape(residues.shape[::-1], F32), shape(rates.shape[::-1], F32)),
        scratch_shapes=[pltpu.VMEM((peers * OUT_ROWS, CHUNK), F32), pltpu.VMEM((3, chans, CHUNK), F32),
                        pltpu.VMEM((peers, CHUNK), F32)],
        compiler_params=ROOM, name="unpack",
    )(returned.reshape(peers * OUT_ROWS, CHUNK), out_cot, sums, lanes)
    return (input_grad, out_gate_grad, in_gate_grad, filter_grad.T, residue_grad.T, rate_grad.T)


def solution(mesh):
    return jax.shard_map(
        local,
        mesh=mesh,
        in_specs=(
            P("ctx", "ch"),
            P("ctx", "ch"),
            P("ctx", "ch"),
            P("ctx", "ch"),
            P(None, "ch"),
            P(None, ("ch", "ctx")),
            P(None, ("ch", "ctx")),
        ),
        out_specs=(
            P("ctx", "ch"),
            P("ctx", "ch"),
            P("ctx", "ch"),
            P(None, "ch"),
            P(None, ("ch", "ctx")),
            P(None, ("ch", "ctx")),
        ),
        check_vma=False,
    )
```

```python
import math

import jax
import jax.numpy as jnp
from jax import lax
from jax.experimental import pallas as pl
from jax.experimental.pallas import tpu as pltpu
from jax.sharding import PartitionSpec as P

F32 = jnp.float32
BF16 = jnp.bfloat16
CHUNK = 128
OWN = 4
MODES = 16
LANES = 128
IN_ROWS = 3 * OWN
OUT_ROWS = 3 * OWN + 2
NT = (((1,), (1,)), ((), ()))
TN = (((0,), (0,)), ((), ()))


def dot(left, right, dims=(((1,), (0,)), ((), ()))):
    return lax.dot_general(left, right, dims, preferred_element_type=F32)


def iota(shape, axis):
    return lax.broadcasted_iota(jnp.int32, shape, axis)


def halves(value):
    high = value.astype(BF16)
    return high, (value - high.astype(F32)).astype(BF16)


def rounded(value):
    return value.astype(BF16).astype(F32)


def mirrored(value):
    square = (value.shape[1], value.shape[1])
    flip = (iota(square, 0) + iota(square, 1) == value.shape[1] - 1).astype(BF16)
    return dot(value, flip).astype(BF16)


def diagonal_sums(square):
    rolled = pltpu.roll(square, 1, 1, stride=1, stride_axis=0)
    return jnp.sum(rolled, axis=0, keepdims=True)


def causal(square):
    return iota(square, 0) + iota(square, 1) >= square[0] - 1


def own_lanes(shape, channel):
    return (iota(shape, 1) % (OWN * MODES)) // MODES == channel


def pick_own(table, count):
    total = jnp.zeros((count, LANES), F32)
    for channel in range(OWN):
        part = table[channel * count : (channel + 1) * count]
        total = total + jnp.where(own_lanes(part.shape, channel), part, 0.0)
    return total


def pack_into(x, k, q, dy, out_ref):
    tiles = (x.shape[1] // 8, 8, x.shape[0])
    gated = rounded(q.astype(F32) * dy.astype(F32))
    x = x.astype(F32).T.reshape(tiles)
    k = pltpu.roll(k.astype(F32).T.reshape(tiles), 4, 1)
    d = gated.T.reshape(tiles)
    low = iota(tiles, 1) < 4
    rows = jnp.stack([jnp.where(low, x, k), jnp.where(low, d, x), jnp.where(low, k, d)], axis=1)
    out_ref[...] = rows.reshape(out_ref.shape).astype(BF16)


def front_kernel(*refs):
    sources, results, held, done = refs[:7], refs[7:18], refs[18:25], refs[25]
    copies = [pltpu.make_async_copy(sources[i], held[i], done.at[i]) for i in range(len(sources))]
    large, small = copies[:4], copies[4:]
    for copy in small + large:
        copy.start()
    for copy in small:
        copy.wait()
    x_ref, k_ref, q_ref, dy_ref, rates_ref, residues_ref, filt_ref = held
    (out_ref, fwd_ref, bwd_ref, hf_ref, hb_ref, aa_ref, bb_ref, g_ref, w_ref,
     e_ref, lanes_ref) = results

    def spread(ref):
        columns = ref[...].T
        return jnp.concatenate(
            [jnp.broadcast_to(columns[:, c : c + 1], (MODES, LANES)) for c in range(OWN)], axis=0
        )

    square = (CHUNK, CHUNK)
    row, lane = iota(square, 0), iota(square, 1)
    upper = lane >= row
    rates, residues = spread(rates_ref), spread(residues_ref)
    weights = residues * jnp.sqrt(2.0 * rates / MODES)
    shape = rates.shape
    step = iota(shape, 1).astype(F32)
    diagonal = iota(shape, 0) == iota(shape, 1) % (OWN * MODES)
    lanes_ref[0:1, :] = jnp.sum(jnp.where(diagonal, rates, 0.0), axis=0, keepdims=True)
    lanes_ref[1:2, :] = jnp.sum(jnp.where(diagonal, residues, 0.0), axis=0, keepdims=True)
    lanes_ref[2:8, :] = jnp.zeros((6, LANES), F32)
    decay = jnp.exp(-rates * step)
    after = jnp.exp(-rates * (step + 1.0))
    before = jnp.exp(-rates * (CHUNK - 1.0 - step))
    high, low = halves(jnp.concatenate([decay, decay * step], axis=0))
    e_ref[...] = jnp.concatenate([high, low], axis=1)

    def wide(value):
        high, low = halves(value)
        return jnp.concatenate([jnp.concatenate([high, low], axis=1)] * 2, axis=0)

    aa_ref[...] = jnp.concatenate([wide(before), wide(before * (CHUNK - 1.0 - step))], axis=0)
    bb_ref[...] = jnp.concatenate([wide(after), wide(after * (step + 1.0))], axis=0)

    def tall(value):
        high, low = halves(value)
        return jnp.concatenate([high, high, low, low], axis=0)

    g_ref[...] = tall(weights * after)
    w_ref[...] = tall(weights * before)
    terms = weights * decay
    for c in range(OWN):
        filt = jnp.sum(terms[c * MODES : (c + 1) * MODES], axis=0, keepdims=True)
        band = pltpu.roll(jnp.broadcast_to(filt, square), 0, 1, stride=1, stride_axis=0)
        high, low = halves(jnp.where(upper, band, 0.0))
        hf_ref[c] = jnp.concatenate([high, low], axis=0)
        hb_ref[c] = jnp.concatenate([high, low], axis=1)
    share = lax.axis_size("ctx") // filt_ref.shape[0]
    group = lax.axis_index("ctx") // share
    pick = (iota((8, filt_ref.shape[0]), 1) == group).astype(BF16)
    taps = dot(pick, filt_ref[...])[0:1]
    band = pltpu.roll(jnp.broadcast_to(taps, square), 0, 1, stride=1, stride_axis=0)
    same = jnp.where(upper, band, 0.0).astype(BF16)
    last = jnp.where(upper, 0.0, band).astype(BF16)
    fwd_ref[...] = jnp.concatenate([same, last], axis=0)
    bwd_ref[...] = jnp.concatenate([same, last], axis=1)
    for copy in large:
        copy.wait()
    pack_into(x_ref[...], k_ref[...], q_ref[...], dy_ref[...], out_ref)


def main_kernel(in_ref, fwd_ref, bwd_ref, hf_ref, hb_ref, aa_ref, bb_ref, g_ref, w_ref,
                e_ref, lanes_ref, out_ref, sums_ref, in32, out32):
    count = in_ref.shape[0] // IN_ROWS
    rows = OWN * count
    in32[...] = in_ref[...].astype(F32)

    def take(which):
        return jnp.concatenate(
            [in32[pl.ds(which * OWN + c, count, stride=IN_ROWS), :] for c in range(OWN)], axis=0
        )

    def put(which, value):
        for c in range(OWN):
            out32[pl.ds(which * OWN + c, count, stride=OUT_ROWS), :] = value[c * count : (c + 1) * count]

    x, k, d = take(0), take(1), take(2)
    place = iota((rows, CHUNK), 0) % count
    x_last = jnp.where(place == 0, 0.0, pltpu.roll(x, 1, 0))
    xx = jnp.concatenate([x.astype(BF16), x_last.astype(BF16)], axis=1)
    v = rounded(dot(xx, fwd_ref[...]))
    u = (k * v).astype(BF16)
    d = d.astype(BF16)
    uu = jnp.concatenate([u, u], axis=1)
    dd = jnp.concatenate([d, d], axis=1)
    moment_u = dot(uu, aa_ref[...], NT)
    moment_d = dot(dd, bb_ref[...], NT)
    slope_u, slope_d = moment_u[:, LANES:], moment_d[:, LANES:]
    moment_u = pick_own(moment_u[:, :LANES], count)
    moment_d = pick_own(moment_d[:, :LANES], count)
    at = iota((count, LANES), 0)
    rates = lanes_ref[0:1, :]
    ahead = jnp.where(at < 1, 0.0, pltpu.roll(moment_u, 1, 0))
    behind = jnp.where(at >= count - 1, 0.0, pltpu.roll(moment_d, count - 1, 0))
    by = 1
    while by < count:
        factor = jnp.exp(rates * (-float(CHUNK) * by))
        ahead = ahead + factor * jnp.where(at < by, 0.0, pltpu.roll(ahead, by, 0))
        behind = behind + factor * jnp.where(at >= count - by, 0.0, pltpu.roll(behind, count - by, 0))
        by *= 2

    def states(value):
        high = rounded(value)
        both = jnp.where(iota(value.shape, 1) < LANES // 2, high, value - high)
        parts = [jnp.where(own_lanes(value.shape, c), both, 0.0) for c in range(OWN)]
        stacked = jnp.concatenate(parts, axis=0).astype(BF16)
        return jnp.concatenate([stacked, stacked], axis=1)

    z = dot(states(ahead), g_ref[...])
    du = dot(states(behind), w_ref[...])
    z_own, du_own = [], []
    for c in range(OWN):
        part = slice(c * count, (c + 1) * count)
        z_own.append(z[part] + dot(uu[part], hf_ref[c]))
        du_own.append(du[part] + dot(dd[part], hb_ref[c], NT))
    put(0, jnp.concatenate(z_own, axis=0))
    du = rounded(jnp.concatenate(du_own, axis=0))
    put(1, du * v)
    dv = rounded(du * k)
    dv_next = jnp.where(place == count - 1, 0.0, pltpu.roll(dv, rows - 1, 0))
    dv = dv.astype(BF16)
    dvv = jnp.concatenate([dv, dv_next.astype(BF16)], axis=1)
    put(2, dot(dvv, bwd_ref[...], NT))
    cross = dot(dv, jnp.concatenate([mirrored(xx[:, :CHUNK]), mirrored(xx[:, CHUNK:])], axis=1), TN)
    sums = diagonal_sums(jnp.where(causal((CHUNK, CHUNK)), cross[:, :CHUNK], cross[:, CHUNK:]))
    high = rounded(sums)
    out32[pl.ds(3 * OWN, count, stride=OUT_ROWS), :] = jnp.broadcast_to(high, (count, CHUNK))
    out32[pl.ds(3 * OWN + 1, count, stride=OUT_ROWS), :] = jnp.broadcast_to(sums - high, (count, CHUNK))
    out_ref[...] = out32[...].astype(BF16)
    first, second = mode_sums(u, d, ahead, behind, moment_d, slope_u, slope_d, e_ref, lanes_ref)
    sums_ref[...] = jnp.concatenate([first, second, jnp.zeros((6, LANES), F32)], axis=0)


def mode_sums(u, d, ahead, behind, moment_d, slope_u, slope_d, e_ref, lanes_ref):
    count = ahead.shape[0]
    keep = causal((CHUNK, CHUNK))
    u_mirrored = mirrored(u)
    cots = []
    for c in range(OWN):
        part = slice(c * count, (c + 1) * count)
        cots.append(diagonal_sums(jnp.where(keep, dot(d[part], u_mirrored[part], TN), 0.0)))
    cots = jnp.concatenate(cots, axis=0)
    high = rounded(cots)
    cots = jnp.concatenate([high, cots - high], axis=0).astype(BF16)
    inner = dot(jnp.concatenate([cots, cots], axis=1), e_ref[...], NT)
    inner = jnp.where((iota(inner.shape, 1) % (OWN * MODES)) // MODES == iota(inner.shape, 0) % OWN, inner, 0.0)
    inner = jnp.sum(inner, axis=0, keepdims=True)
    slope_u, slope_d = pick_own(slope_u, count), pick_own(slope_d, count)
    rates = lanes_ref[0:1, :]
    first = jnp.sum(ahead * moment_d, axis=0, keepdims=True)
    second = jnp.sum(
        ahead * slope_d + slope_u * behind + (CHUNK * jnp.exp(-CHUNK * rates)) * (ahead * behind),
        axis=0, keepdims=True,
    )
    half = iota((1, LANES), 1) < LANES // 2
    first = first + jnp.where(half, inner, pltpu.roll(inner, LANES // 2, 1))
    second = second + jnp.where(half, pltpu.roll(inner, LANES // 2, 1), inner)
    return first, second


def mode_results(scale, sums_ref, lanes_ref, residue_ref, rate_ref):
    first, second = sums_ref[0:1, :], sums_ref[1:2, :]
    rates, residues = lanes_ref[0:1, :], lanes_ref[1:2, :]
    norm = jnp.sqrt(2.0 * rates / MODES)
    results = ((residue_ref, norm * first * scale),
               (rate_ref, residues * norm * (0.5 * first - rates * second) * scale))
    for ref, value in results:
        for c in range(OWN):
            ref[c : c + 1, :] = value[:, c * MODES : (c + 1) * MODES]


def unpack_kernel(scale, in_ref, dy_ref, sums_ref, lanes_ref, dx_ref, dq_ref, dk_ref, filt_ref,
                  residue_ref, rate_ref, in32, mid32, sum32):
    mode_results(scale, sums_ref, lanes_ref, residue_ref, rate_ref)
    count = in_ref.shape[0] // OUT_ROWS
    in32[...] = in_ref[...].astype(F32)

    def take(which):
        for c in range(OWN):
            mid32[which, pl.ds(c, count, stride=OWN), :] = in32[pl.ds(which * OWN + c, count, stride=OUT_ROWS), :]
        return mid32[which].T

    dq_ref[...] = (take(0) * dy_ref[...].astype(F32)).astype(BF16)
    dk_ref[...] = take(1).astype(BF16)
    dx_ref[...] = take(2).astype(BF16)
    sum32[...] = in32[pl.ds(3 * OWN, count, stride=OUT_ROWS), :] + in32[pl.ds(3 * OWN + 1, count, stride=OUT_ROWS), :]
    groups = filt_ref.shape[0]
    share = count // groups
    total = sum32[pl.ds(0, groups, stride=share), :]
    for i in range(1, share):
        total = total + sum32[pl.ds(i, groups, stride=share), :]
    filt_ref[...] = total * scale


ROOM = pltpu.CompilerParams(vmem_limit_bytes=8 * 1024 * 1024)


def shape(dims, kind):
    return jax.ShapeDtypeStruct(dims, kind)


def local(x, out_gate, in_gate, out_cot, mr_filter, residues, rates):
    tokens, chans = x.shape
    peers = lax.axis_size("ctx")
    scale = 1.0 / math.sqrt(tokens * peers)
    square2 = (CHUNK, 2 * CHUNK)
    tall2 = (2 * CHUNK, CHUNK)

    sources = (x, in_gate, out_gate, out_cot, rates.T, residues.T, mr_filter.T)
    packed, fwd, bwd, hf, hb, aa, bb, g, w, e, lanes = pl.pallas_call(
        front_kernel,
        out_shape=(
            shape((peers * IN_ROWS, CHUNK), BF16), shape(tall2, BF16), shape(square2, BF16),
            shape((OWN,) + tall2, BF16), shape((OWN,) + square2, BF16),
            shape((2 * CHUNK, 2 * CHUNK), BF16), shape((2 * CHUNK, 2 * CHUNK), BF16),
            shape(tall2, BF16), shape(tall2, BF16),
            shape(square2, BF16), shape((8, LANES), F32),
        ),
        in_specs=[pl.BlockSpec(memory_space=pltpu.HBM)] * len(sources),
        scratch_shapes=[pltpu.VMEM(source.shape, source.dtype) for source in sources]
        + [pltpu.SemaphoreType.DMA((len(sources),))],
        compiler_params=ROOM, name="front",
    )(*[pltpu.with_memory_space_constraint(source, pltpu.HBM) for source in sources])
    arrived = lax.all_to_all(packed.reshape(3 * peers, OWN, CHUNK), "ctx", split_axis=0, concat_axis=0, tiled=True)

    back, sums = pl.pallas_call(
        main_kernel,
        out_shape=(shape((peers * OUT_ROWS, CHUNK), BF16), shape((8, LANES), F32)),
        scratch_shapes=[pltpu.VMEM((peers * IN_ROWS, CHUNK), F32), pltpu.VMEM((peers * OUT_ROWS, CHUNK), F32)],
        compiler_params=ROOM, name="mixer",
    )(arrived.reshape(peers * IN_ROWS, CHUNK), fwd, bwd, hf, hb, aa, bb, g, w, e, lanes)

    returned = lax.all_to_all(back.reshape(peers * OUT_ROWS // 2, 2, CHUNK), "ctx", split_axis=0, concat_axis=0, tiled=True)

    input_grad, out_gate_grad, in_gate_grad, filter_grad, residue_grad, rate_grad = pl.pallas_call(
        lambda *refs: unpack_kernel(scale, *refs),
        out_shape=(shape(x.shape, BF16), shape(x.shape, BF16), shape(x.shape, BF16),
                   shape(mr_filter.shape[::-1], F32),
                   shape(residues.shape[::-1], F32), shape(rates.shape[::-1], F32)),
        scratch_shapes=[pltpu.VMEM((peers * OUT_ROWS, CHUNK), F32), pltpu.VMEM((3, chans, CHUNK), F32),
                        pltpu.VMEM((peers, CHUNK), F32)],
        compiler_params=ROOM, name="unpack",
    )(returned.reshape(peers * OUT_ROWS, CHUNK), out_cot, sums, lanes)
    return (input_grad, out_gate_grad, in_gate_grad, filter_grad.T, residue_grad.T, rate_grad.T)


def solution(mesh):
    return jax.shard_map(
        local,
        mesh=mesh,
        in_specs=(
            P("ctx", "ch"),
            P("ctx", "ch"),
            P("ctx", "ch"),
            P("ctx", "ch"),
            P(None, "ch"),
            P(None, ("ch", "ctx")),
            P(None, ("ch", "ctx")),
        ),
        out_specs=(
            P("ctx", "ch"),
            P("ctx", "ch"),
            P("ctx", "ch"),
            P(None, "ch"),
            P(None, ("ch", "ctx")),
            P(None, ("ch", "ctx")),
        ),
        check_vma=False,
    )
```

```python
import math

import jax
import jax.numpy as jnp
from jax import lax
from jax.experimental import pallas as pl
from jax.experimental.pallas import tpu as pltpu
from jax.sharding import PartitionSpec as P

F32 = jnp.float32
BF16 = jnp.bfloat16
CHUNK = 128
OWN = 4
MODES = 16
LANES = 128
IN_ROWS = 3 * OWN
OUT_ROWS = 3 * OWN + 2
NT = (((1,), (1,)), ((), ()))
TN = (((0,), (0,)), ((), ()))


def dot(left, right, dims=(((1,), (0,)), ((), ()))):
    return lax.dot_general(left, right, dims, preferred_element_type=F32)


def iota(shape, axis):
    return lax.broadcasted_iota(jnp.int32, shape, axis)


def halves(value):
    high = value.astype(BF16)
    return high, (value - high.astype(F32)).astype(BF16)


def rounded(value):
    return value.astype(BF16).astype(F32)


def mirrored(value):
    square = (value.shape[1], value.shape[1])
    flip = (iota(square, 0) + iota(square, 1) == value.shape[1] - 1).astype(BF16)
    return dot(value, flip).astype(BF16)


def diagonal_sums(square):
    rolled = pltpu.roll(square, 1, 1, stride=1, stride_axis=0)
    return jnp.sum(rolled, axis=0, keepdims=True)


def causal(square):
    return iota(square, 0) + iota(square, 1) >= square[0] - 1


def own_lanes(shape, channel):
    return (iota(shape, 1) % (OWN * MODES)) // MODES == channel


def pick_own(table, count):
    total = jnp.zeros((count, LANES), F32)
    for channel in range(OWN):
        part = table[channel * count : (channel + 1) * count]
        total = total + jnp.where(own_lanes(part.shape, channel), part, 0.0)
    return total


def pack_into(x, k, q, dy, out_ref):
    tiles = (x.shape[1] // 8, 8, x.shape[0])
    gated = (q.astype(F32) * dy.astype(F32)).astype(BF16)
    x = x.T.astype(F32).reshape(tiles)
    k = pltpu.roll(k.T.astype(F32).reshape(tiles), 4, 1)
    d = gated.T.astype(F32).reshape(tiles)
    low = iota(tiles, 1) < 4
    rows = jnp.stack([jnp.where(low, x, k), jnp.where(low, d, x), jnp.where(low, k, d)], axis=1)
    out_ref[...] = rows.reshape(out_ref.shape).astype(BF16)


def front_kernel(*refs):
    sources, results, held, done = refs[:7], refs[7:18], refs[18:25], refs[25]
    copies = [pltpu.make_async_copy(sources[i], held[i], done.at[i]) for i in range(len(sources))]
    large, small = copies[:4], copies[4:]
    for copy in small + large:
        copy.start()
    for copy in small:
        copy.wait()
    x_ref, k_ref, q_ref, dy_ref, rates_ref, residues_ref, filt_ref = held
    (out_ref, fwd_ref, bwd_ref, hf_ref, hb_ref, aa_ref, bb_ref, g_ref, w_ref,
     e_ref, lanes_ref) = results

    def spread(ref):
        columns = ref[...].T
        return jnp.concatenate(
            [jnp.broadcast_to(columns[:, c : c + 1], (MODES, LANES)) for c in range(OWN)], axis=0
        )

    square = (CHUNK, CHUNK)
    row, lane = iota(square, 0), iota(square, 1)
    upper = lane >= row
    rates, residues = spread(rates_ref), spread(residues_ref)
    weights = residues * jnp.sqrt(2.0 * rates / MODES)
    shape = rates.shape
    step = iota(shape, 1).astype(F32)
    diagonal = iota(shape, 0) == iota(shape, 1) % (OWN * MODES)
    lanes_ref[0:1, :] = jnp.sum(jnp.where(diagonal, rates, 0.0), axis=0, keepdims=True)
    lanes_ref[1:2, :] = jnp.sum(jnp.where(diagonal, residues, 0.0), axis=0, keepdims=True)
    lanes_ref[2:8, :] = jnp.zeros((6, LANES), F32)
    decay = jnp.exp(-rates * step)
    after = jnp.exp(-rates * (step + 1.0))
    before = jnp.exp(-rates * (CHUNK - 1.0 - step))
    high, low = halves(jnp.concatenate([decay, decay * step], axis=0))
    e_ref[...] = jnp.concatenate([high, low], axis=1)

    def wide(value):
        high, low = halves(value)
        return jnp.concatenate([jnp.concatenate([high, low], axis=1)] * 2, axis=0)

    aa_ref[...] = jnp.concatenate([wide(before), wide(before * (CHUNK - 1.0 - step))], axis=0)
    bb_ref[...] = jnp.concatenate([wide(after), wide(after * (step + 1.0))], axis=0)

    def tall(value):
        high, low = halves(value)
        return jnp.concatenate([high, high, low, low], axis=0)

    g_ref[...] = tall(weights * after)
    w_ref[...] = tall(weights * before)
    terms = weights * decay
    for c in range(OWN):
        filt = jnp.sum(terms[c * MODES : (c + 1) * MODES], axis=0, keepdims=True)
        band = pltpu.roll(jnp.broadcast_to(filt, square), 0, 1, stride=1, stride_axis=0)
        high, low = halves(jnp.where(upper, band, 0.0))
        hf_ref[c] = jnp.concatenate([high, low], axis=0)
        hb_ref[c] = jnp.concatenate([high, low], axis=1)
    share = lax.axis_size("ctx") // filt_ref.shape[0]
    group = lax.axis_index("ctx") // share
    pick = (iota((8, filt_ref.shape[0]), 1) == group).astype(BF16)
    taps = dot(pick, filt_ref[...])[0:1]
    band = pltpu.roll(jnp.broadcast_to(taps, square), 0, 1, stride=1, stride_axis=0)
    same = jnp.where(upper, band, 0.0).astype(BF16)
    last = jnp.where(upper, 0.0, band).astype(BF16)
    fwd_ref[...] = jnp.concatenate([same, last], axis=0)
    bwd_ref[...] = jnp.concatenate([same, last], axis=1)
    for copy in large:
        copy.wait()
    pack_into(x_ref[...], k_ref[...], q_ref[...], dy_ref[...], out_ref)


def main_kernel(in_ref, fwd_ref, bwd_ref, hf_ref, hb_ref, aa_ref, bb_ref, g_ref, w_ref,
                e_ref, lanes_ref, out_ref, sums_ref, in32, out32):
    count = in_ref.shape[0] // IN_ROWS
    rows = OWN * count
    in32[...] = in_ref[...].astype(F32)

    def take(which):
        return jnp.concatenate(
            [in32[pl.ds(which * OWN + c, count, stride=IN_ROWS), :] for c in range(OWN)], axis=0
        )

    def put(which, value):
        for c in range(OWN):
            out32[pl.ds(which * OWN + c, count, stride=OUT_ROWS), :] = value[c * count : (c + 1) * count]

    x, k, d = take(0), take(1), take(2)
    place = iota((rows, CHUNK), 0) % count
    x_last = jnp.where(place == 0, 0.0, pltpu.roll(x, 1, 0))
    xx = jnp.concatenate([x.astype(BF16), x_last.astype(BF16)], axis=1)
    v = rounded(dot(xx, fwd_ref[...]))
    u = (k * v).astype(BF16)
    d = d.astype(BF16)
    uu = jnp.concatenate([u, u], axis=1)
    dd = jnp.concatenate([d, d], axis=1)
    moment_u = dot(uu, aa_ref[...], NT)
    moment_d = dot(dd, bb_ref[...], NT)
    slope_u, slope_d = moment_u[:, LANES:], moment_d[:, LANES:]
    moment_u = pick_own(moment_u[:, :LANES], count)
    moment_d = pick_own(moment_d[:, :LANES], count)
    at = iota((count, LANES), 0)
    rates = lanes_ref[0:1, :]
    ahead = jnp.where(at < 1, 0.0, pltpu.roll(moment_u, 1, 0))
    behind = jnp.where(at >= count - 1, 0.0, pltpu.roll(moment_d, count - 1, 0))
    by = 1
    while by < count:
        factor = jnp.exp(rates * (-float(CHUNK) * by))
        ahead = ahead + factor * jnp.where(at < by, 0.0, pltpu.roll(ahead, by, 0))
        behind = behind + factor * jnp.where(at >= count - by, 0.0, pltpu.roll(behind, count - by, 0))
        by *= 2

    def states(value):
        high = rounded(value)
        both = jnp.where(iota(value.shape, 1) < LANES // 2, high, value - high)
        parts = [jnp.where(own_lanes(value.shape, c), both, 0.0) for c in range(OWN)]
        stacked = jnp.concatenate(parts, axis=0).astype(BF16)
        return jnp.concatenate([stacked, stacked], axis=1)

    z = dot(states(ahead), g_ref[...])
    du = dot(states(behind), w_ref[...])
    z_own, du_own = [], []
    for c in range(OWN):
        part = slice(c * count, (c + 1) * count)
        z_own.append(z[part] + dot(uu[part], hf_ref[c]))
        du_own.append(du[part] + dot(dd[part], hb_ref[c], NT))
    put(0, jnp.concatenate(z_own, axis=0))
    du = rounded(jnp.concatenate(du_own, axis=0))
    put(1, du * v)
    dv = rounded(du * k)
    dv_next = jnp.where(place == count - 1, 0.0, pltpu.roll(dv, rows - 1, 0))
    dv = dv.astype(BF16)
    dvv = jnp.concatenate([dv, dv_next.astype(BF16)], axis=1)
    put(2, dot(dvv, bwd_ref[...], NT))
    cross = dot(dv, jnp.concatenate([mirrored(xx[:, :CHUNK]), mirrored(xx[:, CHUNK:])], axis=1), TN)
    sums = diagonal_sums(jnp.where(causal((CHUNK, CHUNK)), cross[:, :CHUNK], cross[:, CHUNK:]))
    high = rounded(sums)
    out32[pl.ds(3 * OWN, count, stride=OUT_ROWS), :] = jnp.broadcast_to(high, (count, CHUNK))
    out32[pl.ds(3 * OWN + 1, count, stride=OUT_ROWS), :] = jnp.broadcast_to(sums - high, (count, CHUNK))
    out_ref[...] = out32[...].astype(BF16)
    first, second = mode_sums(u, d, ahead, behind, moment_d, slope_u, slope_d, e_ref, lanes_ref)
    sums_ref[...] = jnp.concatenate([first, second, jnp.zeros((6, LANES), F32)], axis=0)


def mode_sums(u, d, ahead, behind, moment_d, slope_u, slope_d, e_ref, lanes_ref):
    count = ahead.shape[0]
    keep = causal((CHUNK, CHUNK))
    u_mirrored = mirrored(u)
    cots = []
    for c in range(OWN):
        part = slice(c * count, (c + 1) * count)
        cots.append(diagonal_sums(jnp.where(keep, dot(d[part], u_mirrored[part], TN), 0.0)))
    cots = jnp.concatenate(cots, axis=0)
    high = rounded(cots)
    cots = jnp.concatenate([high, cots - high], axis=0).astype(BF16)
    inner = dot(jnp.concatenate([cots, cots], axis=1), e_ref[...], NT)
    inner = jnp.where((iota(inner.shape, 1) % (OWN * MODES)) // MODES == iota(inner.shape, 0) % OWN, inner, 0.0)
    inner = jnp.sum(inner, axis=0, keepdims=True)
    slope_u, slope_d = pick_own(slope_u, count), pick_own(slope_d, count)
    rates = lanes_ref[0:1, :]
    first = jnp.sum(ahead * moment_d, axis=0, keepdims=True)
    second = jnp.sum(
        ahead * slope_d + slope_u * behind + (CHUNK * jnp.exp(-CHUNK * rates)) * (ahead * behind),
        axis=0, keepdims=True,
    )
    half = iota((1, LANES), 1) < LANES // 2
    first = first + jnp.where(half, inner, pltpu.roll(inner, LANES // 2, 1))
    second = second + jnp.where(half, pltpu.roll(inner, LANES // 2, 1), inner)
    return first, second


def mode_results(scale, sums_ref, lanes_ref, residue_ref, rate_ref):
    first, second = sums_ref[0:1, :], sums_ref[1:2, :]
    rates, residues = lanes_ref[0:1, :], lanes_ref[1:2, :]
    norm = jnp.sqrt(2.0 * rates / MODES)
    results = ((residue_ref, norm * first * scale),
               (rate_ref, residues * norm * (0.5 * first - rates * second) * scale))
    for ref, value in results:
        for c in range(OWN):
            ref[c : c + 1, :] = value[:, c * MODES : (c + 1) * MODES]


def unpack_kernel(scale, in_ref, dy_ref, sums_ref, lanes_ref, dx_ref, dq_ref, dk_ref, filt_ref,
                  residue_ref, rate_ref, in32, mid32, sum32):
    mode_results(scale, sums_ref, lanes_ref, residue_ref, rate_ref)
    count = in_ref.shape[0] // OUT_ROWS
    in32[...] = in_ref[...].astype(F32)

    def take(which):
        for c in range(OWN):
            mid32[which, pl.ds(c, count, stride=OWN), :] = in32[pl.ds(which * OWN + c, count, stride=OUT_ROWS), :]
        return mid32[which].astype(BF16).T

    dq_ref[...] = (take(0).astype(F32) * dy_ref[...].astype(F32)).astype(BF16)
    dk_ref[...] = take(1)
    dx_ref[...] = take(2)
    sum32[...] = in32[pl.ds(3 * OWN, count, stride=OUT_ROWS), :] + in32[pl.ds(3 * OWN + 1, count, stride=OUT_ROWS), :]
    groups = filt_ref.shape[0]
    share = count // groups
    total = sum32[pl.ds(0, groups, stride=share), :]
    for i in range(1, share):
        total = total + sum32[pl.ds(i, groups, stride=share), :]
    filt_ref[...] = total * scale


ROOM = pltpu.CompilerParams(vmem_limit_bytes=8 * 1024 * 1024)


def shape(dims, kind):
    return jax.ShapeDtypeStruct(dims, kind)


def local(x, out_gate, in_gate, out_cot, mr_filter, residues, rates):
    tokens, chans = x.shape
    peers = lax.axis_size("ctx")
    scale = 1.0 / math.sqrt(tokens * peers)
    square2 = (CHUNK, 2 * CHUNK)
    tall2 = (2 * CHUNK, CHUNK)

    sources = (x, in_gate, out_gate, out_cot, rates.T, residues.T, mr_filter.T)
    packed, fwd, bwd, hf, hb, aa, bb, g, w, e, lanes = pl.pallas_call(
        front_kernel,
        out_shape=(
            shape((peers * IN_ROWS, CHUNK), BF16), shape(tall2, BF16), shape(square2, BF16),
            shape((OWN,) + tall2, BF16), shape((OWN,) + square2, BF16),
            shape((2 * CHUNK, 2 * CHUNK), BF16), shape((2 * CHUNK, 2 * CHUNK), BF16),
            shape(tall2, BF16), shape(tall2, BF16),
            shape(square2, BF16), shape((8, LANES), F32),
        ),
        in_specs=[pl.BlockSpec(memory_space=pltpu.HBM)] * len(sources),
        scratch_shapes=[pltpu.VMEM(source.shape, source.dtype) for source in sources]
        + [pltpu.SemaphoreType.DMA((len(sources),))],
        compiler_params=ROOM, name="front",
    )(*[pltpu.with_memory_space_constraint(source, pltpu.HBM) for source in sources])
    arrived = lax.all_to_all(packed.reshape(3 * peers, OWN, CHUNK), "ctx", split_axis=0, concat_axis=0, tiled=True)

    back, sums = pl.pallas_call(
        main_kernel,
        out_shape=(shape((peers * OUT_ROWS, CHUNK), BF16), shape((8, LANES), F32)),
        scratch_shapes=[pltpu.VMEM((peers * IN_ROWS, CHUNK), F32), pltpu.VMEM((peers * OUT_ROWS, CHUNK), F32)],
        compiler_params=ROOM, name="mixer",
    )(arrived.reshape(peers * IN_ROWS, CHUNK), fwd, bwd, hf, hb, aa, bb, g, w, e, lanes)

    returned = lax.all_to_all(back.reshape(peers * OUT_ROWS // 2, 2, CHUNK), "ctx", split_axis=0, concat_axis=0, tiled=True)

    input_grad, out_gate_grad, in_gate_grad, filter_grad, residue_grad, rate_grad = pl.pallas_call(
        lambda *refs: unpack_kernel(scale, *refs),
        out_shape=(shape(x.shape, BF16), shape(x.shape, BF16), shape(x.shape, BF16),
                   shape(mr_filter.shape[::-1], F32),
                   shape(residues.shape[::-1], F32), shape(rates.shape[::-1], F32)),
        scratch_shapes=[pltpu.VMEM((peers * OUT_ROWS, CHUNK), F32), pltpu.VMEM((3, chans, CHUNK), F32),
                        pltpu.VMEM((peers, CHUNK), F32)],
        compiler_params=ROOM, name="unpack",
    )(returned.reshape(peers * OUT_ROWS, CHUNK), out_cot, sums, lanes)
    return (input_grad, out_gate_grad, in_gate_grad, filter_grad.T, residue_grad.T, rate_grad.T)


def solution(mesh):
    return jax.shard_map(
        local,
        mesh=mesh,
        in_specs=(
            P("ctx", "ch"),
            P("ctx", "ch"),
            P("ctx", "ch"),
            P("ctx", "ch"),
            P(None, "ch"),
            P(None, ("ch", "ctx")),
            P(None, ("ch", "ctx")),
        ),
        out_specs=(
            P("ctx", "ch"),
            P("ctx", "ch"),
            P("ctx", "ch"),
            P(None, "ch"),
            P(None, ("ch", "ctx")),
            P(None, ("ch", "ctx")),
        ),
        check_vma=False,
    )
```

```python
import math

import jax
import jax.numpy as jnp
from jax import lax
from jax.experimental import pallas as pl
from jax.experimental.pallas import tpu as pltpu
from jax.sharding import PartitionSpec as P

F32 = jnp.float32
BF16 = jnp.bfloat16
CHUNK = 128
OWN = 4
MODES = 16
LANES = 128
IN_ROWS = 3 * OWN
OUT_ROWS = 3 * OWN + 2
NT = (((1,), (1,)), ((), ()))
TN = (((0,), (0,)), ((), ()))


def dot(left, right, dims=(((1,), (0,)), ((), ()))):
    return lax.dot_general(left, right, dims, preferred_element_type=F32)


def iota(shape, axis):
    return lax.broadcasted_iota(jnp.int32, shape, axis)


def halves(value):
    high = value.astype(BF16)
    return high, (value - high.astype(F32)).astype(BF16)


def rounded(value):
    return value.astype(BF16).astype(F32)


def mirrored(value):
    square = (value.shape[1], value.shape[1])
    flip = (iota(square, 0) + iota(square, 1) == value.shape[1] - 1).astype(BF16)
    return dot(value, flip).astype(BF16)


def diagonal_sums(square):
    rolled = pltpu.roll(square, 1, 1, stride=1, stride_axis=0)
    return jnp.sum(rolled, axis=0, keepdims=True)


def causal(square):
    return iota(square, 0) + iota(square, 1) >= square[0] - 1


def own_lanes(shape, channel):
    return (iota(shape, 1) % (OWN * MODES)) // MODES == channel


def fold(value):
    half = value.shape[1] // 2
    return value[:, :half] + value[:, half:]


def pick_own(table, count):
    total = jnp.zeros((count, LANES), F32)
    for channel in range(OWN):
        part = table[channel * count : (channel + 1) * count]
        total = total + jnp.where(own_lanes(part.shape, channel), part, 0.0)
    return total


def pack_into(x, k, q, dy, out_ref):
    tiles = (x.shape[1] // 8, 8, x.shape[0])
    gated = rounded(q.astype(F32) * dy.astype(F32))
    x = x.astype(F32).T.reshape(tiles)
    k = pltpu.roll(k.astype(F32).T.reshape(tiles), 4, 1)
    d = gated.T.reshape(tiles)
    low = iota(tiles, 1) < 4
    rows = jnp.stack([jnp.where(low, x, k), jnp.where(low, d, x), jnp.where(low, k, d)], axis=1)
    out_ref[...] = rows.reshape(out_ref.shape).astype(BF16)


def front_kernel(*refs):
    sources, results, held, done = refs[:7], refs[7:17], refs[17:24], refs[24]
    copies = [pltpu.make_async_copy(sources[i], held[i], done.at[i]) for i in range(len(sources))]
    large, small = copies[:4], copies[4:]
    for copy in small + large:
        copy.start()
    for copy in small:
        copy.wait()
    x_ref, k_ref, q_ref, dy_ref, rates_ref, residues_ref, filt_ref = held
    (out_ref, fwd_ref, bwd_ref, hf_ref, aa_ref, bb_ref, g_ref, w_ref,
     e_ref, lanes_ref) = results

    def spread(ref):
        columns = ref[...].T
        return jnp.concatenate(
            [jnp.broadcast_to(columns[:, c : c + 1], (MODES, LANES)) for c in range(OWN)], axis=0
        )

    square = (CHUNK, CHUNK)
    row, lane = iota(square, 0), iota(square, 1)
    upper = lane >= row
    rates, residues = spread(rates_ref), spread(residues_ref)
    weights = residues * jnp.sqrt(2.0 * rates / MODES)
    shape = rates.shape
    step = iota(shape, 1).astype(F32)
    diagonal = iota(shape, 0) == iota(shape, 1) % (OWN * MODES)
    lanes_ref[0:1, :] = jnp.sum(jnp.where(diagonal, rates, 0.0), axis=0, keepdims=True)
    lanes_ref[1:2, :] = jnp.sum(jnp.where(diagonal, residues, 0.0), axis=0, keepdims=True)
    lanes_ref[2:8, :] = jnp.zeros((6, LANES), F32)
    decay = jnp.exp(-rates * step)
    after = jnp.exp(-rates * (step + 1.0))
    before = jnp.exp(-rates * (CHUNK - 1.0 - step))
    high, low = halves(jnp.concatenate([decay, decay * step], axis=0))
    e_ref[...] = jnp.concatenate([high, low], axis=1)

    def wide(value):
        high, low = halves(value)
        return jnp.concatenate([jnp.concatenate([high, low], axis=1)] * 2, axis=0)

    aa_ref[...] = jnp.concatenate([wide(before), wide(before * (CHUNK - 1.0 - step))], axis=0)
    bb_ref[...] = jnp.concatenate([wide(after), wide(after * (step + 1.0))], axis=0)

    def tall(value):
        high, low = halves(value)
        return jnp.concatenate([high, high, low, low], axis=0)

    g_ref[...] = tall(weights * after)
    w_ref[...] = tall(weights * before)
    terms = weights * decay
    for c in range(OWN):
        filt = jnp.sum(terms[c * MODES : (c + 1) * MODES], axis=0, keepdims=True)
        band = pltpu.roll(jnp.broadcast_to(filt, square), 0, 1, stride=1, stride_axis=0)
        high, low = halves(jnp.where(upper, band, 0.0))
        hf_ref[c] = jnp.concatenate([high, low], axis=0)
    share = lax.axis_size("ctx") // filt_ref.shape[0]
    group = lax.axis_index("ctx") // share
    pick = (iota((8, filt_ref.shape[0]), 1) == group).astype(BF16)
    taps = dot(pick, filt_ref[...])[0:1]
    band = pltpu.roll(jnp.broadcast_to(taps, square), 0, 1, stride=1, stride_axis=0)
    same = jnp.where(upper, band, 0.0).astype(BF16)
    last = jnp.where(upper, 0.0, band).astype(BF16)
    fwd_ref[...] = jnp.concatenate([same, last], axis=0)
    bwd_ref[...] = jnp.concatenate([same, last], axis=1)
    for copy in large:
        copy.wait()
    pack_into(x_ref[...], k_ref[...], q_ref[...], dy_ref[...], out_ref)


def main_kernel(in_ref, fwd_ref, bwd_ref, hf_ref, aa_ref, bb_ref, g_ref, w_ref,
                e_ref, lanes_ref, out_ref, sums_ref, in32, out32):
    count = in_ref.shape[0] // IN_ROWS
    rows = OWN * count
    in32[...] = in_ref[...].astype(F32)

    def take(which):
        return jnp.concatenate(
            [in32[pl.ds(which * OWN + c, count, stride=IN_ROWS), :] for c in range(OWN)], axis=0
        )

    def put(which, value):
        for c in range(OWN):
            out32[pl.ds(which * OWN + c, count, stride=OUT_ROWS), :] = value[c * count : (c + 1) * count]

    x, k, d = take(0), take(1), take(2)
    place = iota((rows, CHUNK), 0) % count
    x_last = jnp.where(place == 0, 0.0, pltpu.roll(x, 1, 0))
    xx = jnp.concatenate([x.astype(BF16), x_last.astype(BF16)], axis=1)
    v = rounded(dot(xx, fwd_ref[...]))
    u = (k * v).astype(BF16)
    d = d.astype(BF16)
    uu = jnp.concatenate([u, u], axis=1)
    dd = jnp.concatenate([d, d], axis=1)
    moment_u = dot(uu, aa_ref[...], NT)
    moment_d = dot(dd, bb_ref[...], NT)
    slope_u, slope_d = moment_u[:, LANES:], moment_d[:, LANES:]
    moment_u = pick_own(moment_u[:, :LANES], count)
    moment_d = pick_own(moment_d[:, :LANES], count)
    at = iota((count, LANES), 0)
    rates = lanes_ref[0:1, :]
    ahead = jnp.where(at < 1, 0.0, pltpu.roll(moment_u, 1, 0))
    behind = jnp.where(at >= count - 1, 0.0, pltpu.roll(moment_d, count - 1, 0))
    by = 1
    while by < count:
        factor = jnp.exp(rates * (-float(CHUNK) * by))
        ahead = ahead + factor * jnp.where(at < by, 0.0, pltpu.roll(ahead, by, 0))
        behind = behind + factor * jnp.where(at >= count - by, 0.0, pltpu.roll(behind, count - by, 0))
        by *= 2

    def states(value):
        high = rounded(value)
        both = jnp.where(iota(value.shape, 1) < LANES // 2, high, value - high)
        parts = [jnp.where(own_lanes(value.shape, c), both, 0.0) for c in range(OWN)]
        stacked = jnp.concatenate(parts, axis=0).astype(BF16)
        return jnp.concatenate([stacked, stacked], axis=1)

    z = dot(states(ahead), g_ref[...])
    du = dot(states(behind), w_ref[...])
    z_own, du_own = [], []
    for c in range(OWN):
        part = slice(c * count, (c + 1) * count)
        z_own.append(z[part] + dot(uu[part], hf_ref[c]))
        du_own.append(du[part] + fold(dot(d[part], hf_ref[c], NT)))
    put(0, jnp.concatenate(z_own, axis=0))
    du = rounded(jnp.concatenate(du_own, axis=0))
    put(1, du * v)
    dv = rounded(du * k)
    dv_next = jnp.where(place == count - 1, 0.0, pltpu.roll(dv, rows - 1, 0))
    dv = dv.astype(BF16)
    dvv = jnp.concatenate([dv, dv_next.astype(BF16)], axis=1)
    put(2, dot(dvv, bwd_ref[...], NT))
    cross = dot(dv, jnp.concatenate([mirrored(xx[:, :CHUNK]), mirrored(xx[:, CHUNK:])], axis=1), TN)
    sums = diagonal_sums(jnp.where(causal((CHUNK, CHUNK)), cross[:, :CHUNK], cross[:, CHUNK:]))
    high = rounded(sums)
    out32[pl.ds(3 * OWN, count, stride=OUT_ROWS), :] = jnp.broadcast_to(high, (count, CHUNK))
    out32[pl.ds(3 * OWN + 1, count, stride=OUT_ROWS), :] = jnp.broadcast_to(sums - high, (count, CHUNK))
    out_ref[...] = out32[...].astype(BF16)
    first, second = mode_sums(u, d, ahead, behind, moment_d, slope_u, slope_d, e_ref, lanes_ref)
    sums_ref[...] = jnp.concatenate([first, second, jnp.zeros((6, LANES), F32)], axis=0)


def mode_sums(u, d, ahead, behind, moment_d, slope_u, slope_d, e_ref, lanes_ref):
    count = ahead.shape[0]
    keep = causal((CHUNK, CHUNK))
    u_mirrored = mirrored(u)
    cots = []
    for c in range(OWN):
        part = slice(c * count, (c + 1) * count)
        cots.append(diagonal_sums(jnp.where(keep, dot(d[part], u_mirrored[part], TN), 0.0)))
    cots = jnp.concatenate(cots, axis=0)
    high = rounded(cots)
    cots = jnp.concatenate([high, cots - high], axis=0).astype(BF16)
    inner = dot(jnp.concatenate([cots, cots], axis=1), e_ref[...], NT)
    inner = jnp.where((iota(inner.shape, 1) % (OWN * MODES)) // MODES == iota(inner.shape, 0) % OWN, inner, 0.0)
    inner = jnp.sum(inner, axis=0, keepdims=True)
    slope_u, slope_d = pick_own(slope_u, count), pick_own(slope_d, count)
    rates = lanes_ref[0:1, :]
    first = jnp.sum(ahead * moment_d, axis=0, keepdims=True)
    second = jnp.sum(
        ahead * slope_d + slope_u * behind + (CHUNK * jnp.exp(-CHUNK * rates)) * (ahead * behind),
        axis=0, keepdims=True,
    )
    half = iota((1, LANES), 1) < LANES // 2
    first = first + jnp.where(half, inner, pltpu.roll(inner, LANES // 2, 1))
    second = second + jnp.where(half, pltpu.roll(inner, LANES // 2, 1), inner)
    return first, second


def mode_results(scale, sums_ref, lanes_ref, residue_ref, rate_ref):
    first, second = sums_ref[0:1, :], sums_ref[1:2, :]
    rates, residues = lanes_ref[0:1, :], lanes_ref[1:2, :]
    norm = jnp.sqrt(2.0 * rates / MODES)
    results = ((residue_ref, norm * first * scale),
               (rate_ref, residues * norm * (0.5 * first - rates * second) * scale))
    for ref, value in results:
        for c in range(OWN):
            ref[c : c + 1, :] = value[:, c * MODES : (c + 1) * MODES]


def unpack_kernel(scale, in_ref, dy_ref, sums_ref, lanes_ref, dx_ref, dq_ref, dk_ref, filt_ref,
                  residue_ref, rate_ref, in32, mid32, sum32):
    mode_results(scale, sums_ref, lanes_ref, residue_ref, rate_ref)
    count = in_ref.shape[0] // OUT_ROWS
    in32[...] = in_ref[...].astype(F32)

    def take(which):
        for c in range(OWN):
            mid32[which, pl.ds(c, count, stride=OWN), :] = in32[pl.ds(which * OWN + c, count, stride=OUT_ROWS), :]
        return mid32[which].T

    dq_ref[...] = (take(0) * dy_ref[...].astype(F32)).astype(BF16)
    dk_ref[...] = take(1).astype(BF16)
    dx_ref[...] = take(2).astype(BF16)
    sum32[...] = in32[pl.ds(3 * OWN, count, stride=OUT_ROWS), :] + in32[pl.ds(3 * OWN + 1, count, stride=OUT_ROWS), :]
    groups = filt_ref.shape[0]
    share = count // groups
    total = sum32[pl.ds(0, groups, stride=share), :]
    for i in range(1, share):
        total = total + sum32[pl.ds(i, groups, stride=share), :]
    filt_ref[...] = total * scale


ROOM = pltpu.CompilerParams(vmem_limit_bytes=8 * 1024 * 1024)


def shape(dims, kind):
    return jax.ShapeDtypeStruct(dims, kind)


def local(x, out_gate, in_gate, out_cot, mr_filter, residues, rates):
    tokens, chans = x.shape
    peers = lax.axis_size("ctx")
    scale = 1.0 / math.sqrt(tokens * peers)
    square2 = (CHUNK, 2 * CHUNK)
    tall2 = (2 * CHUNK, CHUNK)

    sources = (x, in_gate, out_gate, out_cot, rates.T, residues.T, mr_filter.T)
    packed, fwd, bwd, hf, aa, bb, g, w, e, lanes = pl.pallas_call(
        front_kernel,
        out_shape=(
            shape((peers * IN_ROWS, CHUNK), BF16), shape(tall2, BF16), shape(square2, BF16),
            shape((OWN,) + tall2, BF16),
            shape((2 * CHUNK, 2 * CHUNK), BF16), shape((2 * CHUNK, 2 * CHUNK), BF16),
            shape(tall2, BF16), shape(tall2, BF16),
            shape(square2, BF16), shape((8, LANES), F32),
        ),
        in_specs=[pl.BlockSpec(memory_space=pltpu.HBM)] * len(sources),
        scratch_shapes=[pltpu.VMEM(source.shape, source.dtype) for source in sources]
        + [pltpu.SemaphoreType.DMA((len(sources),))],
        compiler_params=ROOM, name="front",
    )(*[pltpu.with_memory_space_constraint(source, pltpu.HBM) for source in sources])
    arrived = lax.all_to_all(packed.reshape(3 * peers, OWN, CHUNK), "ctx", split_axis=0, concat_axis=0, tiled=True)

    back, sums = pl.pallas_call(
        main_kernel,
        out_shape=(shape((peers * OUT_ROWS, CHUNK), BF16), shape((8, LANES), F32)),
        scratch_shapes=[pltpu.VMEM((peers * IN_ROWS, CHUNK), F32), pltpu.VMEM((peers * OUT_ROWS, CHUNK), F32)],
        compiler_params=ROOM, name="mixer",
    )(arrived.reshape(peers * IN_ROWS, CHUNK), fwd, bwd, hf, aa, bb, g, w, e, lanes)

    returned = lax.all_to_all(back.reshape(peers * OUT_ROWS // 2, 2, CHUNK), "ctx", split_axis=0, concat_axis=0, tiled=True)

    input_grad, out_gate_grad, in_gate_grad, filter_grad, residue_grad, rate_grad = pl.pallas_call(
        lambda *refs: unpack_kernel(scale, *refs),
        out_shape=(shape(x.shape, BF16), shape(x.shape, BF16), shape(x.shape, BF16),
                   shape(mr_filter.shape[::-1], F32),
                   shape(residues.shape[::-1], F32), shape(rates.shape[::-1], F32)),
        scratch_shapes=[pltpu.VMEM((peers * OUT_ROWS, CHUNK), F32), pltpu.VMEM((3, chans, CHUNK), F32),
                        pltpu.VMEM((peers, CHUNK), F32)],
        compiler_params=ROOM, name="unpack",
    )(returned.reshape(peers * OUT_ROWS, CHUNK), out_cot, sums, lanes)
    return (input_grad, out_gate_grad, in_gate_grad, filter_grad.T, residue_grad.T, rate_grad.T)


def solution(mesh):
    return jax.shard_map(
        local,
        mesh=mesh,
        in_specs=(
            P("ctx", "ch"),
            P("ctx", "ch"),
            P("ctx", "ch"),
            P("ctx", "ch"),
            P(None, "ch"),
            P(None, ("ch", "ctx")),
            P(None, ("ch", "ctx")),
        ),
        out_specs=(
            P("ctx", "ch"),
            P("ctx", "ch"),
            P("ctx", "ch"),
            P(None, "ch"),
            P(None, ("ch", "ctx")),
            P(None, ("ch", "ctx")),
        ),
        check_vma=False,
    )
```

```python
import math

import jax
import jax.numpy as jnp
from jax import lax
from jax.experimental import pallas as pl
from jax.experimental.pallas import tpu as pltpu
from jax.sharding import PartitionSpec as P

F32 = jnp.float32
BF16 = jnp.bfloat16
CHUNK = 128
OWN = 4
MODES = 16
LANES = 128
IN_ROWS = 3 * OWN
OUT_ROWS = 3 * OWN + 2
NT = (((1,), (1,)), ((), ()))
TN = (((0,), (0,)), ((), ()))


def dot(left, right, dims=(((1,), (0,)), ((), ()))):
    return lax.dot_general(left, right, dims, preferred_element_type=F32)


def iota(shape, axis):
    return lax.broadcasted_iota(jnp.int32, shape, axis)


def halves(value):
    high = value.astype(BF16)
    return high, (value - high.astype(F32)).astype(BF16)


def rounded(value):
    return value.astype(BF16).astype(F32)


def mirrored(value):
    square = (value.shape[1], value.shape[1])
    flip = (iota(square, 0) + iota(square, 1) == value.shape[1] - 1).astype(BF16)
    return dot(value, flip).astype(BF16)


def diagonal_sums(square):
    rolled = pltpu.roll(square, 1, 1, stride=1, stride_axis=0)
    return jnp.sum(rolled, axis=0, keepdims=True)


def causal(square):
    return iota(square, 0) + iota(square, 1) >= square[0] - 1


def own_lanes(shape, channel):
    return (iota(shape, 1) % (OWN * MODES)) // MODES == channel


def pick_own(table, count):
    total = jnp.zeros((count, LANES), F32)
    for channel in range(OWN):
        part = table[channel * count : (channel + 1) * count]
        total = total + jnp.where(own_lanes(part.shape, channel), part, 0.0)
    return total


def pack_into(x, k, q, dy, out_ref):
    tiles = (x.shape[1] // 8, 8, x.shape[0])
    gated = rounded(q.astype(F32) * dy.astype(F32))
    x = x.astype(F32).T.reshape(tiles)
    k = pltpu.roll(k.astype(F32).T.reshape(tiles), 4, 1)
    d = gated.T.reshape(tiles)
    low = iota(tiles, 1) < 4
    rows = jnp.stack([jnp.where(low, x, k), jnp.where(low, d, x), jnp.where(low, k, d)], axis=1)
    out_ref[...] = rows.reshape(out_ref.shape).astype(BF16)


def front_kernel(*refs):
    sources, results, held, done = refs[:7], refs[7:18], refs[18:25], refs[25]
    copies = [pltpu.make_async_copy(sources[i], held[i], done.at[i]) for i in range(len(sources))]
    large, small = copies[:4], copies[4:]
    for copy in small + large:
        copy.start()
    for copy in small:
        copy.wait()
    x_ref, k_ref, q_ref, dy_ref, rates_ref, residues_ref, filt_ref = held
    (out_ref, fwd_ref, bwd_ref, hf_ref, hb_ref, aa_ref, bb_ref, g_ref, w_ref,
     e_ref, lanes_ref) = results

    def spread(ref):
        columns = ref[...].T
        return jnp.concatenate(
            [jnp.broadcast_to(columns[:, c : c + 1], (MODES, LANES)) for c in range(OWN)], axis=0
        )

    square = (CHUNK, CHUNK)
    row, lane = iota(square, 0), iota(square, 1)
    upper = lane >= row
    rates, residues = spread(rates_ref), spread(residues_ref)
    weights = residues * jnp.sqrt(2.0 * rates / MODES)
    shape = rates.shape
    step = iota(shape, 1).astype(F32)
    diagonal = iota(shape, 0) == iota(shape, 1) % (OWN * MODES)
    lanes_ref[0:1, :] = jnp.sum(jnp.where(diagonal, rates, 0.0), axis=0, keepdims=True)
    lanes_ref[1:2, :] = jnp.sum(jnp.where(diagonal, residues, 0.0), axis=0, keepdims=True)
    lanes_ref[2:8, :] = jnp.zeros((6, LANES), F32)
    decay = jnp.exp(-rates * step)
    after = decay * jnp.exp(-rates)
    before = jnp.exp(-rates * (CHUNK - 1.0 - step))
    high, low = halves(jnp.concatenate([decay, decay * step], axis=0))
    e_ref[...] = jnp.concatenate([high, low], axis=1)

    def wide(value):
        high, low = halves(value)
        return jnp.concatenate([jnp.concatenate([high, low], axis=1)] * 2, axis=0)

    aa_ref[...] = jnp.concatenate([wide(before), wide(before * (CHUNK - 1.0 - step))], axis=0)
    bb_ref[...] = jnp.concatenate([wide(after), wide(after * (step + 1.0))], axis=0)

    def tall(value):
        high, low = halves(value)
        return jnp.concatenate([high, high, low, low], axis=0)

    g_ref[...] = tall(weights * after)
    w_ref[...] = tall(weights * before)
    terms = weights * decay
    for c in range(OWN):
        filt = jnp.sum(terms[c * MODES : (c + 1) * MODES], axis=0, keepdims=True)
        band = pltpu.roll(jnp.broadcast_to(filt, square), 0, 1, stride=1, stride_axis=0)
        high, low = halves(jnp.where(upper, band, 0.0))
        hf_ref[c] = jnp.concatenate([high, low], axis=0)
        hb_ref[c] = jnp.concatenate([high, low], axis=1)
    share = lax.axis_size("ctx") // filt_ref.shape[0]
    group = lax.axis_index("ctx") // share
    pick = (iota((8, filt_ref.shape[0]), 1) == group).astype(BF16)
    taps = dot(pick, filt_ref[...])[0:1]
    band = pltpu.roll(jnp.broadcast_to(taps, square), 0, 1, stride=1, stride_axis=0)
    same = jnp.where(upper, band, 0.0).astype(BF16)
    last = jnp.where(upper, 0.0, band).astype(BF16)
    fwd_ref[...] = jnp.concatenate([same, last], axis=0)
    bwd_ref[...] = jnp.concatenate([same, last], axis=1)
    for copy in large:
        copy.wait()
    pack_into(x_ref[...], k_ref[...], q_ref[...], dy_ref[...], out_ref)


def main_kernel(in_ref, fwd_ref, bwd_ref, hf_ref, hb_ref, aa_ref, bb_ref, g_ref, w_ref,
                e_ref, lanes_ref, out_ref, sums_ref, in32, out32):
    count = in_ref.shape[0] // IN_ROWS
    rows = OWN * count
    in32[...] = in_ref[...].astype(F32)

    def take(which):
        return jnp.concatenate(
            [in32[pl.ds(which * OWN + c, count, stride=IN_ROWS), :] for c in range(OWN)], axis=0
        )

    def put(which, value):
        for c in range(OWN):
            out32[pl.ds(which * OWN + c, count, stride=OUT_ROWS), :] = value[c * count : (c + 1) * count]

    x, k, d = take(0), take(1), take(2)
    place = iota((rows, CHUNK), 0) % count
    x_last = jnp.where(place == 0, 0.0, pltpu.roll(x, 1, 0))
    xx = jnp.concatenate([x.astype(BF16), x_last.astype(BF16)], axis=1)
    v = rounded(dot(xx, fwd_ref[...]))
    u = (k * v).astype(BF16)
    d = d.astype(BF16)
    uu = jnp.concatenate([u, u], axis=1)
    dd = jnp.concatenate([d, d], axis=1)
    moment_u = dot(uu, aa_ref[...], NT)
    moment_d = dot(dd, bb_ref[...], NT)
    slope_u, slope_d = moment_u[:, LANES:], moment_d[:, LANES:]
    moment_u = pick_own(moment_u[:, :LANES], count)
    moment_d = pick_own(moment_d[:, :LANES], count)
    at = iota((count, LANES), 0)
    rates = lanes_ref[0:1, :]
    ahead = jnp.where(at < 1, 0.0, pltpu.roll(moment_u, 1, 0))
    behind = jnp.where(at >= count - 1, 0.0, pltpu.roll(moment_d, count - 1, 0))
    by = 1
    while by < count:
        factor = jnp.exp(rates * (-float(CHUNK) * by))
        ahead = ahead + factor * jnp.where(at < by, 0.0, pltpu.roll(ahead, by, 0))
        behind = behind + factor * jnp.where(at >= count - by, 0.0, pltpu.roll(behind, count - by, 0))
        by *= 2

    def states(value):
        high = rounded(value)
        both = jnp.where(iota(value.shape, 1) < LANES // 2, high, value - high).astype(BF16)
        none = jnp.zeros_like(both)
        stacked = jnp.concatenate([jnp.where(own_lanes(value.shape, c), both, none) for c in range(OWN)], axis=0)
        return jnp.concatenate([stacked, stacked], axis=1)

    z = dot(states(ahead), g_ref[...])
    du = dot(states(behind), w_ref[...])
    z_own, du_own = [], []
    for c in range(OWN):
        part = slice(c * count, (c + 1) * count)
        z_own.append(z[part] + dot(uu[part], hf_ref[c]))
        du_own.append(du[part] + dot(dd[part], hb_ref[c], NT))
    put(0, jnp.concatenate(z_own, axis=0))
    du = rounded(jnp.concatenate(du_own, axis=0))
    put(1, du * v)
    dv = rounded(du * k)
    dv_next = jnp.where(place == count - 1, 0.0, pltpu.roll(dv, rows - 1, 0))
    dv = dv.astype(BF16)
    dvv = jnp.concatenate([dv, dv_next.astype(BF16)], axis=1)
    put(2, dot(dvv, bwd_ref[...], NT))
    cross = dot(dv, jnp.concatenate([mirrored(xx[:, :CHUNK]), mirrored(xx[:, CHUNK:])], axis=1), TN)
    sums = diagonal_sums(jnp.where(causal((CHUNK, CHUNK)), cross[:, :CHUNK], cross[:, CHUNK:]))
    high = rounded(sums)
    out32[pl.ds(3 * OWN, count, stride=OUT_ROWS), :] = jnp.broadcast_to(high, (count, CHUNK))
    out32[pl.ds(3 * OWN + 1, count, stride=OUT_ROWS), :] = jnp.broadcast_to(sums - high, (count, CHUNK))
    out_ref[...] = out32[...].astype(BF16)
    first, second = mode_sums(u, d, ahead, behind, moment_d, slope_u, slope_d, e_ref, lanes_ref)
    sums_ref[...] = jnp.concatenate([first, second, jnp.zeros((6, LANES), F32)], axis=0)


def mode_sums(u, d, ahead, behind, moment_d, slope_u, slope_d, e_ref, lanes_ref):
    count = ahead.shape[0]
    keep = causal((CHUNK, CHUNK))
    u_mirrored = mirrored(u)
    cots = []
    for c in range(OWN):
        part = slice(c * count, (c + 1) * count)
        cots.append(diagonal_sums(jnp.where(keep, dot(d[part], u_mirrored[part], TN), 0.0)))
    cots = jnp.concatenate(cots, axis=0)
    high = rounded(cots)
    cots = jnp.concatenate([high, cots - high], axis=0).astype(BF16)
    inner = dot(jnp.concatenate([cots, cots], axis=1), e_ref[...], NT)
    inner = jnp.where((iota(inner.shape, 1) % (OWN * MODES)) // MODES == iota(inner.shape, 0) % OWN, inner, 0.0)
    inner = jnp.sum(inner, axis=0, keepdims=True)
    slope_u, slope_d = pick_own(slope_u, count), pick_own(slope_d, count)
    rates = lanes_ref[0:1, :]
    first = jnp.sum(ahead * moment_d, axis=0, keepdims=True)
    second = jnp.sum(
        ahead * slope_d + slope_u * behind + (CHUNK * jnp.exp(-CHUNK * rates)) * (ahead * behind),
        axis=0, keepdims=True,
    )
    half = iota((1, LANES), 1) < LANES // 2
    first = first + jnp.where(half, inner, pltpu.roll(inner, LANES // 2, 1))
    second = second + jnp.where(half, pltpu.roll(inner, LANES // 2, 1), inner)
    return first, second


def mode_results(scale, sums_ref, lanes_ref, residue_ref, rate_ref):
    first, second = sums_ref[0:1, :], sums_ref[1:2, :]
    rates, residues = lanes_ref[0:1, :], lanes_ref[1:2, :]
    norm = jnp.sqrt(2.0 * rates / MODES)
    results = ((residue_ref, norm * first * scale),
               (rate_ref, residues * norm * (0.5 * first - rates * second) * scale))
    for ref, value in results:
        for c in range(OWN):
            ref[c : c + 1, :] = value[:, c * MODES : (c + 1) * MODES]


def unpack_kernel(scale, in_ref, dy_ref, sums_ref, lanes_ref, dx_ref, dq_ref, dk_ref, filt_ref,
                  residue_ref, rate_ref, in32, mid32, sum32):
    mode_results(scale, sums_ref, lanes_ref, residue_ref, rate_ref)
    count = in_ref.shape[0] // OUT_ROWS
    in32[...] = in_ref[...].astype(F32)

    def take(which):
        for c in range(OWN):
            mid32[which, pl.ds(c, count, stride=OWN), :] = in32[pl.ds(which * OWN + c, count, stride=OUT_ROWS), :]
        return mid32[which].T

    dq_ref[...] = (take(0) * dy_ref[...].astype(F32)).astype(BF16)
    dk_ref[...] = take(1).astype(BF16)
    dx_ref[...] = take(2).astype(BF16)
    sum32[...] = in32[pl.ds(3 * OWN, count, stride=OUT_ROWS), :] + in32[pl.ds(3 * OWN + 1, count, stride=OUT_ROWS), :]
    groups = filt_ref.shape[0]
    share = count // groups
    total = sum32[pl.ds(0, groups, stride=share), :]
    for i in range(1, share):
        total = total + sum32[pl.ds(i, groups, stride=share), :]
    filt_ref[...] = total * scale


ROOM = pltpu.CompilerParams(vmem_limit_bytes=8 * 1024 * 1024)


def shape(dims, kind):
    return jax.ShapeDtypeStruct(dims, kind)


def local(x, out_gate, in_gate, out_cot, mr_filter, residues, rates):
    tokens, chans = x.shape
    peers = lax.axis_size("ctx")
    scale = 1.0 / math.sqrt(tokens * peers)
    square2 = (CHUNK, 2 * CHUNK)
    tall2 = (2 * CHUNK, CHUNK)

    sources = (x, in_gate, out_gate, out_cot, rates.T, residues.T, mr_filter.T)
    packed, fwd, bwd, hf, hb, aa, bb, g, w, e, lanes = pl.pallas_call(
        front_kernel,
        out_shape=(
            shape((peers * IN_ROWS, CHUNK), BF16), shape(tall2, BF16), shape(square2, BF16),
            shape((OWN,) + tall2, BF16), shape((OWN,) + square2, BF16),
            shape((2 * CHUNK, 2 * CHUNK), BF16), shape((2 * CHUNK, 2 * CHUNK), BF16),
            shape(tall2, BF16), shape(tall2, BF16),
            shape(square2, BF16), shape((8, LANES), F32),
        ),
        in_specs=[pl.BlockSpec(memory_space=pltpu.HBM)] * len(sources),
        scratch_shapes=[pltpu.VMEM(source.shape, source.dtype) for source in sources]
        + [pltpu.SemaphoreType.DMA((len(sources),))],
        compiler_params=ROOM, name="front",
    )(*[pltpu.with_memory_space_constraint(source, pltpu.HBM) for source in sources])
    arrived = lax.all_to_all(packed.reshape(3 * peers, OWN, CHUNK), "ctx", split_axis=0, concat_axis=0, tiled=True)

    back, sums = pl.pallas_call(
        main_kernel,
        out_shape=(shape((peers * OUT_ROWS, CHUNK), BF16), shape((8, LANES), F32)),
        scratch_shapes=[pltpu.VMEM((peers * IN_ROWS, CHUNK), F32), pltpu.VMEM((peers * OUT_ROWS, CHUNK), F32)],
        compiler_params=ROOM, name="mixer",
    )(arrived.reshape(peers * IN_ROWS, CHUNK), fwd, bwd, hf, hb, aa, bb, g, w, e, lanes)

    returned = lax.all_to_all(back.reshape(peers * OUT_ROWS // 2, 2, CHUNK), "ctx", split_axis=0, concat_axis=0, tiled=True)

    input_grad, out_gate_grad, in_gate_grad, filter_grad, residue_grad, rate_grad = pl.pallas_call(
        lambda *refs: unpack_kernel(scale, *refs),
        out_shape=(shape(x.shape, BF16), shape(x.shape, BF16), shape(x.shape, BF16),
                   shape(mr_filter.shape[::-1], F32),
                   shape(residues.shape[::-1], F32), shape(rates.shape[::-1], F32)),
        scratch_shapes=[pltpu.VMEM((peers * OUT_ROWS, CHUNK), F32), pltpu.VMEM((3, chans, CHUNK), F32),
                        pltpu.VMEM((peers, CHUNK), F32)],
        compiler_params=ROOM, name="unpack",
    )(returned.reshape(peers * OUT_ROWS, CHUNK), out_cot, sums, lanes)
    return (input_grad, out_gate_grad, in_gate_grad, filter_grad.T, residue_grad.T, rate_grad.T)


def solution(mesh):
    return jax.shard_map(
        local,
        mesh=mesh,
        in_specs=(
            P("ctx", "ch"),
            P("ctx", "ch"),
            P("ctx", "ch"),
            P("ctx", "ch"),
            P(None, "ch"),
            P(None, ("ch", "ctx")),
            P(None, ("ch", "ctx")),
        ),
        out_specs=(
            P("ctx", "ch"),
            P("ctx", "ch"),
            P("ctx", "ch"),
            P(None, "ch"),
            P(None, ("ch", "ctx")),
            P(None, ("ch", "ctx")),
        ),
        check_vma=False,
    )
```

```python
import math

import jax
import jax.numpy as jnp
from jax import lax
from jax.experimental import pallas as pl
from jax.experimental.pallas import tpu as pltpu
from jax.sharding import PartitionSpec as P

F32 = jnp.float32
BF16 = jnp.bfloat16
CHUNK = 128
OWN = 4
MODES = 16
LANES = 128
IN_ROWS = 3 * OWN
OUT_ROWS = 3 * OWN + 2
NT = (((1,), (1,)), ((), ()))
TN = (((0,), (0,)), ((), ()))


def dot(left, right, dims=(((1,), (0,)), ((), ()))):
    return lax.dot_general(left, right, dims, preferred_element_type=F32)


def iota(shape, axis):
    return lax.broadcasted_iota(jnp.int32, shape, axis)


def halves(value):
    high = value.astype(BF16)
    return high, (value - high.astype(F32)).astype(BF16)


def rounded(value):
    return value.astype(BF16).astype(F32)


def mirrored(value):
    square = (value.shape[1], value.shape[1])
    flip = (iota(square, 0) + iota(square, 1) == value.shape[1] - 1).astype(BF16)
    return dot(value, flip).astype(BF16)


def diagonal_sums(square):
    rolled = pltpu.roll(square, 1, 1, stride=1, stride_axis=0)
    return jnp.sum(rolled, axis=0, keepdims=True)


def causal(square):
    return iota(square, 0) + iota(square, 1) >= square[0] - 1


def own_lanes(shape, channel):
    return (iota(shape, 1) % (OWN * MODES)) // MODES == channel


def pick_own(table, count):
    total = jnp.zeros((count, LANES), F32)
    for channel in range(OWN):
        part = table[channel * count : (channel + 1) * count]
        total = total + jnp.where(own_lanes(part.shape, channel), part, 0.0)
    return total


def pack_into(x, k, q, dy, out_ref):
    tiles = (x.shape[1] // 8, 8, x.shape[0])
    gated = rounded(q.astype(F32) * dy.astype(F32))
    x = x.astype(F32).T.reshape(tiles)
    k = pltpu.roll(k.astype(F32).T.reshape(tiles), 4, 1)
    d = gated.T.reshape(tiles)
    low = iota(tiles, 1) < 4
    rows = jnp.stack([jnp.where(low, x, k), jnp.where(low, d, x), jnp.where(low, k, d)], axis=1)
    out_ref[...] = rows.reshape(out_ref.shape).astype(BF16)


def front_kernel(*refs):
    sources, results, held, done = refs[:7], refs[7:18], refs[18:25], refs[25]
    copies = [pltpu.make_async_copy(sources[i], held[i], done.at[i]) for i in range(len(sources))]
    large, small = copies[:4], copies[4:]
    for copy in small + large:
        copy.start()
    for copy in small:
        copy.wait()
    x_ref, k_ref, q_ref, dy_ref, rates_ref, residues_ref, filt_ref = held
    (out_ref, fwd_ref, bwd_ref, hf_ref, hb_ref, aa_ref, bb_ref, g_ref, w_ref,
     e_ref, lanes_ref) = results

    def spread(ref):
        columns = ref[...].T
        return jnp.concatenate(
            [jnp.broadcast_to(columns[:, c : c + 1], (MODES, LANES)) for c in range(OWN)], axis=0
        )

    square = (CHUNK, CHUNK)
    row, lane = iota(square, 0), iota(square, 1)
    upper = lane >= row
    rates, residues = spread(rates_ref), spread(residues_ref)
    weights = residues * jnp.sqrt(2.0 * rates / MODES)
    shape = rates.shape
    step = iota(shape, 1).astype(F32)
    diagonal = iota(shape, 0) == iota(shape, 1) % (OWN * MODES)
    lanes_ref[0:1, :] = jnp.sum(jnp.where(diagonal, rates, 0.0), axis=0, keepdims=True)
    lanes_ref[1:2, :] = jnp.sum(jnp.where(diagonal, residues, 0.0), axis=0, keepdims=True)
    lanes_ref[2:8, :] = jnp.zeros((6, LANES), F32)
    decay = jnp.exp(-rates * step)
    after = jnp.exp(-rates * (step + 1.0))
    before = jnp.exp(-rates * (CHUNK - 1.0 - step))
    high, low = halves(jnp.concatenate([decay, decay * step], axis=0))
    e_ref[...] = jnp.concatenate([high, low], axis=1)

    def wide(value):
        high, low = halves(value)
        return jnp.concatenate([jnp.concatenate([high, low], axis=1)] * 2, axis=0)

    aa_ref[...] = jnp.concatenate([wide(before), wide(before * (CHUNK - 1.0 - step))], axis=0)
    bb_ref[...] = jnp.concatenate([wide(after), wide(after * (step + 1.0))], axis=0)

    def tall(value):
        high, low = halves(value)
        return jnp.concatenate([high, high, low, low], axis=0)

    g_ref[...] = tall(weights * after)
    w_ref[...] = tall(weights * before)
    terms = weights * decay
    for c in range(OWN):
        filt = jnp.sum(terms[c * MODES : (c + 1) * MODES], axis=0, keepdims=True)
        band = pltpu.roll(jnp.broadcast_to(filt, square), 0, 1, stride=1, stride_axis=0)
        high, low = halves(jnp.where(upper, band, 0.0))
        hf_ref[c] = jnp.concatenate([high, low], axis=0)
        hb_ref[c] = jnp.concatenate([high, low], axis=1)
    share = lax.axis_size("ctx") // filt_ref.shape[0]
    group = lax.axis_index("ctx") // share
    pick = (iota((8, filt_ref.shape[0]), 1) == group).astype(BF16)
    taps = dot(pick, filt_ref[...])[0:1]
    band = pltpu.roll(jnp.broadcast_to(taps, square), 0, 1, stride=1, stride_axis=0)
    same = jnp.where(upper, band, 0.0).astype(BF16)
    last = jnp.where(upper, 0.0, band).astype(BF16)
    fwd_ref[...] = jnp.concatenate([same, last], axis=0)
    bwd_ref[...] = jnp.concatenate([same, last], axis=1)
    for copy in large:
        copy.wait()
    pack_into(x_ref[...], k_ref[...], q_ref[...], dy_ref[...], out_ref)


def main_kernel(in_ref, fwd_ref, bwd_ref, hf_ref, hb_ref, aa_ref, bb_ref, g_ref, w_ref,
                e_ref, lanes_ref, out_ref, sums_ref, in32, out32):
    count = in_ref.shape[0] // IN_ROWS
    rows = OWN * count
    in32[...] = in_ref[...].astype(F32)

    def take(which):
        return jnp.concatenate(
            [in32[pl.ds(which * OWN + c, count, stride=IN_ROWS), :] for c in range(OWN)], axis=0
        )

    def put(which, value):
        for c in range(OWN):
            out32[pl.ds(which * OWN + c, count, stride=OUT_ROWS), :] = value[c * count : (c + 1) * count]

    x, k, d = take(0), take(1), take(2)
    place = iota((rows, CHUNK), 0) % count
    x_last = jnp.where(place == 0, 0.0, pltpu.roll(x, 1, 0))
    xx = jnp.concatenate([x.astype(BF16), x_last.astype(BF16)], axis=1)
    v = rounded(dot(xx, fwd_ref[...]))
    u = (k * v).astype(BF16)
    d = d.astype(BF16)
    uu = jnp.concatenate([u, u], axis=1)
    dd = jnp.concatenate([d, d], axis=1)
    moment_u = dot(uu, aa_ref[...], NT)
    moment_d = dot(dd, bb_ref[...], NT)
    slope_u, slope_d = moment_u[:, LANES:], moment_d[:, LANES:]
    moment_u = pick_own(moment_u[:, :LANES], count)
    moment_d = pick_own(moment_d[:, :LANES], count)
    at = iota((count, LANES), 0)
    rates = lanes_ref[0:1, :]
    ahead = jnp.where(at < 1, 0.0, pltpu.roll(moment_u, 1, 0))
    behind = jnp.where(at >= count - 1, 0.0, pltpu.roll(moment_d, count - 1, 0))
    by = 1
    while by < count:
        factor = jnp.exp(rates * (-float(CHUNK) * by))
        ahead = ahead + factor * jnp.where(at < by, 0.0, pltpu.roll(ahead, by, 0))
        behind = behind + factor * jnp.where(at >= count - by, 0.0, pltpu.roll(behind, count - by, 0))
        by *= 2

    def states(value):
        high = rounded(value)
        both = jnp.where(iota(value.shape, 1) < LANES // 2, high, value - high)
        parts = [jnp.where(own_lanes(value.shape, c), both, 0.0) for c in range(OWN)]
        stacked = jnp.concatenate(parts, axis=0).astype(BF16)
        return jnp.concatenate([stacked, stacked], axis=1)

    z = dot(states(ahead), g_ref[...])
    du = dot(states(behind), w_ref[...])
    z_own, du_own = [], []
    for c in range(OWN):
        part = slice(c * count, (c + 1) * count)
        z_own.append(z[part] + dot(uu[part], hf_ref[c]))
        du_own.append(du[part] + dot(dd[part], hb_ref[c], NT))
    put(0, jnp.concatenate(z_own, axis=0))
    du = rounded(jnp.concatenate(du_own, axis=0))
    put(1, du * v)
    dv = rounded(du * k)
    dv_next = jnp.where(place == count - 1, 0.0, pltpu.roll(dv, rows - 1, 0))
    dv = dv.astype(BF16)
    dvv = jnp.concatenate([dv, dv_next.astype(BF16)], axis=1)
    put(2, dot(dvv, bwd_ref[...], NT))
    cross = dot(jnp.concatenate([mirrored(xx[:, :CHUNK]), mirrored(xx[:, CHUNK:])], axis=1), dv, TN)
    sums = diagonal_sums(jnp.where(causal((CHUNK, CHUNK)), cross[:CHUNK], cross[CHUNK:]))
    high = rounded(sums)
    out32[pl.ds(3 * OWN, count, stride=OUT_ROWS), :] = jnp.broadcast_to(high, (count, CHUNK))
    out32[pl.ds(3 * OWN + 1, count, stride=OUT_ROWS), :] = jnp.broadcast_to(sums - high, (count, CHUNK))
    out_ref[...] = out32[...].astype(BF16)
    first, second = mode_sums(u, d, ahead, behind, moment_d, slope_u, slope_d, e_ref, lanes_ref)
    sums_ref[...] = jnp.concatenate([first, second, jnp.zeros((6, LANES), F32)], axis=0)


def mode_sums(u, d, ahead, behind, moment_d, slope_u, slope_d, e_ref, lanes_ref):
    count = ahead.shape[0]
    keep = causal((CHUNK, CHUNK))
    u_mirrored = mirrored(u)
    cots = []
    for c in range(OWN):
        part = slice(c * count, (c + 1) * count)
        cots.append(diagonal_sums(jnp.where(keep, dot(d[part], u_mirrored[part], TN), 0.0)))
    cots = jnp.concatenate(cots, axis=0)
    high = rounded(cots)
    cots = jnp.concatenate([high, cots - high], axis=0).astype(BF16)
    inner = dot(jnp.concatenate([cots, cots], axis=1), e_ref[...], NT)
    inner = jnp.where((iota(inner.shape, 1) % (OWN * MODES)) // MODES == iota(inner.shape, 0) % OWN, inner, 0.0)
    inner = jnp.sum(inner, axis=0, keepdims=True)
    slope_u, slope_d = pick_own(slope_u, count), pick_own(slope_d, count)
    rates = lanes_ref[0:1, :]
    first = jnp.sum(ahead * moment_d, axis=0, keepdims=True)
    second = jnp.sum(
        ahead * slope_d + slope_u * behind + (CHUNK * jnp.exp(-CHUNK * rates)) * (ahead * behind),
        axis=0, keepdims=True,
    )
    half = iota((1, LANES), 1) < LANES // 2
    first = first + jnp.where(half, inner, pltpu.roll(inner, LANES // 2, 1))
    second = second + jnp.where(half, pltpu.roll(inner, LANES // 2, 1), inner)
    return first, second


def mode_results(scale, sums_ref, lanes_ref, residue_ref, rate_ref):
    first, second = sums_ref[0:1, :], sums_ref[1:2, :]
    rates, residues = lanes_ref[0:1, :], lanes_ref[1:2, :]
    norm = jnp.sqrt(2.0 * rates / MODES)
    results = ((residue_ref, norm * first * scale),
               (rate_ref, residues * norm * (0.5 * first - rates * second) * scale))
    for ref, value in results:
        for c in range(OWN):
            ref[c : c + 1, :] = value[:, c * MODES : (c + 1) * MODES]


def unpack_kernel(scale, in_ref, dy_ref, sums_ref, lanes_ref, dx_ref, dq_ref, dk_ref, filt_ref,
                  residue_ref, rate_ref, in32, mid32, sum32):
    mode_results(scale, sums_ref, lanes_ref, residue_ref, rate_ref)
    count = in_ref.shape[0] // OUT_ROWS
    in32[...] = in_ref[...].astype(F32)

    def take(which):
        for c in range(OWN):
            mid32[which, pl.ds(c, count, stride=OWN), :] = in32[pl.ds(which * OWN + c, count, stride=OUT_ROWS), :]
        return mid32[which].T

    dq_ref[...] = (take(0) * dy_ref[...].astype(F32)).astype(BF16)
    dk_ref[...] = take(1).astype(BF16)
    dx_ref[...] = take(2).astype(BF16)
    sum32[...] = in32[pl.ds(3 * OWN, count, stride=OUT_ROWS), :] + in32[pl.ds(3 * OWN + 1, count, stride=OUT_ROWS), :]
    groups = filt_ref.shape[0]
    share = count // groups
    total = sum32[pl.ds(0, groups, stride=share), :]
    for i in range(1, share):
        total = total + sum32[pl.ds(i, groups, stride=share), :]
    filt_ref[...] = total * scale


ROOM = pltpu.CompilerParams(vmem_limit_bytes=8 * 1024 * 1024)


def shape(dims, kind):
    return jax.ShapeDtypeStruct(dims, kind)


def local(x, out_gate, in_gate, out_cot, mr_filter, residues, rates):
    tokens, chans = x.shape
    peers = lax.axis_size("ctx")
    scale = 1.0 / math.sqrt(tokens * peers)
    square2 = (CHUNK, 2 * CHUNK)
    tall2 = (2 * CHUNK, CHUNK)

    sources = (x, in_gate, out_gate, out_cot, rates.T, residues.T, mr_filter.T)
    packed, fwd, bwd, hf, hb, aa, bb, g, w, e, lanes = pl.pallas_call(
        front_kernel,
        out_shape=(
            shape((peers * IN_ROWS, CHUNK), BF16), shape(tall2, BF16), shape(square2, BF16),
            shape((OWN,) + tall2, BF16), shape((OWN,) + square2, BF16),
            shape((2 * CHUNK, 2 * CHUNK), BF16), shape((2 * CHUNK, 2 * CHUNK), BF16),
            shape(tall2, BF16), shape(tall2, BF16),
            shape(square2, BF16), shape((8, LANES), F32),
        ),
        in_specs=[pl.BlockSpec(memory_space=pltpu.HBM)] * len(sources),
        scratch_shapes=[pltpu.VMEM(source.shape, source.dtype) for source in sources]
        + [pltpu.SemaphoreType.DMA((len(sources),))],
        compiler_params=ROOM, name="front",
    )(*[pltpu.with_memory_space_constraint(source, pltpu.HBM) for source in sources])
    arrived = lax.all_to_all(packed.reshape(3 * peers, OWN, CHUNK), "ctx", split_axis=0, concat_axis=0, tiled=True)

    back, sums = pl.pallas_call(
        main_kernel,
        out_shape=(shape((peers * OUT_ROWS, CHUNK), BF16), shape((8, LANES), F32)),
        scratch_shapes=[pltpu.VMEM((peers * IN_ROWS, CHUNK), F32), pltpu.VMEM((peers * OUT_ROWS, CHUNK), F32)],
        compiler_params=ROOM, name="mixer",
    )(arrived.reshape(peers * IN_ROWS, CHUNK), fwd, bwd, hf, hb, aa, bb, g, w, e, lanes)

    returned = lax.all_to_all(back.reshape(peers * OUT_ROWS // 2, 2, CHUNK), "ctx", split_axis=0, concat_axis=0, tiled=True)

    input_grad, out_gate_grad, in_gate_grad, filter_grad, residue_grad, rate_grad = pl.pallas_call(
        lambda *refs: unpack_kernel(scale, *refs),
        out_shape=(shape(x.shape, BF16), shape(x.shape, BF16), shape(x.shape, BF16),
                   shape(mr_filter.shape[::-1], F32),
                   shape(residues.shape[::-1], F32), shape(rates.shape[::-1], F32)),
        scratch_shapes=[pltpu.VMEM((peers * OUT_ROWS, CHUNK), F32), pltpu.VMEM((3, chans, CHUNK), F32),
                        pltpu.VMEM((peers, CHUNK), F32)],
        compiler_params=ROOM, name="unpack",
    )(returned.reshape(peers * OUT_ROWS, CHUNK), out_cot, sums, lanes)
    return (input_grad, out_gate_grad, in_gate_grad, filter_grad.T, residue_grad.T, rate_grad.T)


def solution(mesh):
    return jax.shard_map(
        local,
        mesh=mesh,
        in_specs=(
            P("ctx", "ch"),
            P("ctx", "ch"),
            P("ctx", "ch"),
            P("ctx", "ch"),
            P(None, "ch"),
            P(None, ("ch", "ctx")),
            P(None, ("ch", "ctx")),
        ),
        out_specs=(
            P("ctx", "ch"),
            P("ctx", "ch"),
            P("ctx", "ch"),
            P(None, "ch"),
            P(None, ("ch", "ctx")),
            P(None, ("ch", "ctx")),
        ),
        check_vma=False,
    )
```
